32 devices in a mesh: ep: 8 (over z, y), rep: 4 (over x, core).
Axes of the slice: x: 2, y: 2, z: 4, core: 2. Of those that a mesh axis runs over, the one named last changes fastest.
Arguments:
- out_grad: bfloat16 [1024, 2048], P(('ep', 'rep')), may hold values from -6 to 6
- gate_weights: float32 [1024, 8], P(('ep', 'rep')), may hold values from 0.05 to 1
- expert_ids: int32 [1024, 8], P(('ep', 'rep')), may hold values from 0 to 15, all different within a row; in each aligned block of 32 rows (0 to 31, 32 to 63, ...) at most 32 rows name the same one
- down_weight: bfloat16 [16, 2048, 384], P('ep'), may hold values from -0.3125 to 0.3125
- act_cache: bfloat16 [16, 1024, 384], P('ep', 'rep'), may hold values from -0.25 to 0.25
Outputs:
- in_grad: bfloat16 [1024, 8, 384], P(('ep', 'rep'))
- weight_grad: bfloat16 [16, 2048, 384], P('ep', 'rep')
The draws below stay inside these ranges and needn't reach their ends.
Inputs may be any that keep to these rules, and one draw needn't show every extreme that they name: `expert_ids`: each row names 8 different experts. Among the tokens of one device (aligned blocks of 32 rows), no expert is named by more than 32 tokens, a bound that some block reaches.
All inputs are finite; a program needn't handle non-finite values.
Results may differ from the reference program's by a relative error of at most 0.014.
Values may be sent and summed in bfloat16 or wider, within the bound.
A program may use at most 64 MiB of HBM per device.

```python
import math
import jax
import jax.numpy as jnp
import numpy as np
from jax import lax

D = 2048
FF = 384
TOPK = 8
EXP_DEV = 2
TOK_DEV = 32
EXPERTS = 16
CAP = 32
SLOTS = 1024
TOKENS = 1024
N_EP = 8
N_REP = 4


def block_scale(rng, dims, cuts, smallest, high):
    factor_of, own = 1.0, jax.random.fold_in(rng, 6)
    for dim, shards_of in cuts:
        steps = jnp.exp(jax.random.uniform(jax.random.fold_in(own, dim), (shards_of,), jnp.float32, smallest / len(cuts), high / len(cuts)))
        factor_of = factor_of * jnp.repeat(steps, dims[dim] // shards_of).reshape([-1 if axis == dim else 1 for axis in range(len(dims))])
    return factor_of


def deal_out(stream_key, own, number, rows, amount, top, bound, slope):
    order = jax.random.permutation(stream_key, amount)
    heavy_load, ordinary = portions_of(amount, rows * top, bound, slope, True), portions_of(amount, rows * top, bound, slope, False)
    places = jnp.arange(amount)

    def named(lengths, rotation):
        used = int((lengths > 0).sum())
        fixed = max(1, used // 4)
        passed = fixed + (places - fixed + rotation * (used - fixed)) % max(1, amount - fixed)
        return jnp.zeros((amount,), jnp.int32).at[order[jnp.where(places < fixed, places, passed)]].set(jnp.asarray(lengths, jnp.int32))

    lengths = jnp.where(number % 4 == 0, named(heavy_load, number // 4), named(ordinary, number - number // 4 - 1))
    mixed = jax.random.permutation(jax.random.fold_in(own, 3), amount)
    donor, sink = mixed[0:amount // 2 * 2:2], mixed[1:amount // 2 * 2:2]
    margin = jnp.minimum(lengths[donor] - 1, bound - lengths[sink]) // 2
    margin = jnp.where((donor == order[0]) | (sink == order[0]) | (lengths[sink] == 0), 0, jnp.maximum(margin, 0))
    passed = jax.random.randint(jax.random.fold_in(own, 4), (amount // 2,), 0, 1 << 20) % (margin + 1)
    lengths = lengths.at[donor].add(-passed).at[sink].add(passed)
    items = jnp.searchsorted(jnp.cumsum(lengths), jnp.arange(rows * top), side="right").astype(jnp.int32)
    listing = items.reshape(top, rows).T
    listing = listing[jax.random.permutation(jax.random.fold_in(own, 1), rows)]
    rotation = jax.random.randint(jax.random.fold_in(own, 2), (rows, 1), 0, top)
    return jnp.take_along_axis(listing, (jnp.arange(top)[None, :] + rotation) % top, axis=1)


def portions_of(count, total, reach, slope, full):
    weights = [(1 << 20) // math.isqrt(standing ** slope) + 1 for standing in range(1, count + 1)]
    largest = reach if full else min(reach, max(-(-total // count), total * weights[0] // sum(weights)))
    least = 1 if total - largest >= count - 1 else 0
    holding, rest = [largest] + [least] * (count - 1), total - largest - least * (count - 1)
    while rest > 0:
        movable = [i for i in range(1, count) if holding[i] < largest] or [i for i in range(1, count) if holding[i] < reach]
        mass, remaining = sum([weights[i] for i in movable]), rest
        for i in movable:
            extra = min(reach - holding[i], max(1, remaining * weights[i] // mass), rest)
            holding[i] = holding[i] + extra
            rest = rest - extra
    return np.array(holding)


def gaussian(key, extent, width, most, cuts=(), held_as=jnp.bfloat16):
    loudness = block_scale(key, extent, cuts, -0.22, 0.18) if cuts else 1.0
    array = jax.random.normal(key, extent, jnp.float32) * width * loudness
    return jnp.minimum(jnp.maximum(array, -most), most).astype(held_as)


def setup_inputs(seed: int = 0) -> dict:
    key_list = jax.random.split(jax.random.key(seed), 6)
    out_grad = gaussian(key_list[0], (TOKENS, D), 1.0, 6.0, ((0, 32),))
    gate_weights = jnp.clip(jnp.exp(math.log(1.0) - 2.9957323 * jax.random.uniform(key_list[1], (TOKENS, TOPK), jnp.float32) ** block_scale(key_list[1], (TOKENS, TOPK), ((0, 32),), -0.2, 0.2)), 0.05, 1.0)
    expert_ids_keys = jax.random.split(jax.random.fold_in(key_list[2], 1), TOKENS // TOK_DEV)
    expert_ids_turns = jax.random.permutation(jax.random.fold_in(key_list[2], 3), TOKENS // TOK_DEV)
    expert_ids = jax.vmap(lambda own, number: deal_out(jax.random.fold_in(key_list[2], 2), own, number, TOK_DEV, EXPERTS, TOPK, CAP, 2))(expert_ids_keys, expert_ids_turns).reshape((TOKENS, TOPK))
    down_weight = gaussian(key_list[3], (EXPERTS, D, FF), FF ** -0.5, 0.3125, ((0, 8),))
    act_cache = gaussian(key_list[4], (EXPERTS, SLOTS, FF), (TOK_DEV * TOPK * N_REP // EXP_DEV) ** -0.5, 0.25, ((0, 8), (1, 4)))
    return dict(out_grad=out_grad, gate_weights=gate_weights, expert_ids=expert_ids, down_weight=down_weight, act_cache=act_cache)


def slots_of(route_block):
    onehot = (route_block[:, :, None] == jnp.arange(EXPERTS, dtype=jnp.int32)[None, None, :]).astype(jnp.int32)
    earlier = jnp.cumsum(onehot, axis=1) - onehot
    return jnp.sum(earlier * onehot, axis=2).astype(jnp.int32)


def reference(out_grad, gate_weights, expert_ids, down_weight, act_cache):
    pair_count = TOK_DEV * TOPK
    grads = out_grad.reshape(N_EP, N_REP, TOK_DEV, D)
    gate_all = gate_weights.reshape(N_EP, N_REP, TOK_DEV, TOPK)
    routes = expert_ids.reshape(N_EP, N_REP, pair_count)
    weight_full = down_weight.astype(jnp.float32)

    def one_replica(carry, index):
        grad_block = lax.dynamic_index_in_dim(grads, index, 1, keepdims=False)
        gate_block = lax.dynamic_index_in_dim(gate_all, index, 1, keepdims=False)
        route_block = lax.dynamic_index_in_dim(routes, index, 1, keepdims=False).astype(jnp.int32)
        pair_grad = (gate_block[..., None] * grad_block.astype(jnp.float32)[:, :, None, :]).astype(jnp.bfloat16)
        pair_grad = pair_grad.reshape(N_EP * pair_count, D)
        slot_block = slots_of(route_block)
        source = jnp.arange(N_EP, dtype=jnp.int32)[:, None]
        position = ((route_block * N_EP + source) * CAP + slot_block).reshape(-1).astype(jnp.int32)
        buffer = jnp.zeros((EXPERTS * N_EP * CAP, D), jnp.bfloat16).at[position].set(pair_grad)
        buffer = buffer.reshape(EXPERTS, N_EP * CAP, D).astype(jnp.float32)
        input_rows = jnp.einsum("erd,edf->erf", buffer, weight_full).astype(jnp.bfloat16)
        input_rows = input_rows.reshape(EXPERTS * N_EP * CAP, FF)
        in_block = input_rows[position].reshape(N_EP, TOK_DEV, TOPK, FF)
        start = (index * (N_EP * CAP)).astype(jnp.int32)
        saved = lax.dynamic_slice_in_dim(act_cache, start, N_EP * CAP, 1).astype(jnp.float32)
        partial_value = jnp.einsum("erd,erf->edf", buffer, saved).astype(jnp.bfloat16)
        partial_value = lax.optimization_barrier(partial_value).astype(jnp.float32)
        return carry + partial_value, in_block

    initial = jnp.zeros((EXPERTS, D, FF), jnp.float32)
    total, blocks = lax.scan(one_replica, initial, jnp.arange(N_REP, dtype=jnp.int32))
    in_grad = jnp.transpose(blocks, (1, 0, 2, 3, 4)).reshape(TOKENS, TOPK, FF)
    return in_grad, total.astype(jnp.bfloat16)
```

```python
import functools
import jax
import jax.numpy as jnp
from jax import lax
from jax.experimental import pallas as pl
from jax.experimental.pallas import tpu as pltpu
from jax.sharding import PartitionSpec as P

MESH = pl.DeviceIdType.MESH
F32 = jnp.float32
BF16 = jnp.bfloat16
INNER = 2
PIECES = 1
GROUP = 8


def kernel(
    n_ep, n_rep, og_hbm, ids_ref, gate_ref, w_hbm, act_hbm, ing_ref, wg_ref,
    xg, xs, rs, actg, wv, yb, rb, acc, at,
    lsem, ag_send, ag_recv, rg_send, rg_recv, act_send, act_recv, fw_send,
    rs_send, rs_recv, rf_send, xs_send, xs_recv, back_send, back_recv,
):
    topk, tok = ids_ref.shape
    model = og_hbm.shape[1]
    loc, _, hid = w_hbm.shape
    experts = loc * n_ep
    width = rs.shape[3]
    part = xs.shape[3]
    cap = act_hbm.shape[1] // n_ep
    outer = n_ep // INNER
    half = model // PIECES
    me = lax.axis_index("ep")
    rep = lax.axis_index("rep")
    zi, yi = me // INNER, lax.rem(me, INNER)
    hi_rep, core = rep // 2, lax.rem(rep, 2)
    halves = n_rep // 2
    cross = [lax.rem(hi_rep + j, halves) * 2 + core for j in range(1, halves)]
    partner = hi_rep * 2 + 1 - core

    barrier = pltpu.get_barrier_semaphore()
    for j in range(1, n_ep):
        pl.semaphore_signal(
            barrier, inc=1, device_id={"ep": lax.rem(me + j, n_ep)}, device_id_type=MESH
        )
    for j in range(1, n_rep):
        pl.semaphore_signal(
            barrier, inc=1, device_id={"rep": lax.rem(rep + j, n_rep)}, device_id_type=MESH
        )

    load_x = pltpu.make_async_copy(og_hbm, xg.at[me], lsem.at[0])
    load_x.start()
    load_a = pltpu.make_async_copy(act_hbm, actg.at[rep], lsem.at[1])
    load_a.start()
    load_w = pltpu.make_async_copy(w_hbm, wv, lsem.at[2])
    load_w.start()

    ids = ids_ref[...]
    gates = gate_ref[...]
    high = gates.astype(BF16).astype(F32)
    low = gates - high
    line = lax.broadcasted_iota(jnp.int32, (width, tok), 0)
    dense = jnp.zeros((width, tok), F32)
    for k in range(topk):
        e_k = ids[k : k + 1, :]
        dense = jnp.where(line == e_k, high[k : k + 1, :], dense)
        dense = jnp.where(line == e_k + experts, low[k : k + 1, :], dense)
    eye_r = lax.broadcasted_iota(jnp.int32, (width, width), 0)
    eye_c = lax.broadcasted_iota(jnp.int32, (width, width), 1)
    eye = jnp.where(eye_r == eye_c, 1.0, 0.0).astype(BF16)
    rs[rep, me] = lax.dot_general(
        dense.astype(BF16), eye, (((0,), (0,)), ((), ())), preferred_element_type=F32
    ).astype(BF16)

    pl.semaphore_wait(barrier, n_ep - 1 + n_rep - 1)

    def begin(copy):
        copy.start()

    def end_send(copy):
        copy.wait_send()

    def rg_copy(j):
        return pltpu.make_async_remote_copy(
            src_ref=rs.at[rep, me], dst_ref=rs.at[rep, me],
            send_sem=rg_send.at[j], recv_sem=rg_recv.at[me],
            device_id={"ep": lax.rem(me + j, n_ep)}, device_id_type=MESH,
        )

    def ag_copy(block, way, piece, target):
        cols = pl.ds(piece * half, half)
        return pltpu.make_async_remote_copy(
            src_ref=xg.at[block, :, cols], dst_ref=xg.at[block, :, cols],
            send_sem=ag_send.at[way, block, piece], recv_sem=ag_recv.at[block, piece],
            device_id={"ep": target}, device_id_type=MESH,
        )

    def ag_arrived(block, piece):
        ag_copy(block, 0, piece, lax.rem(me + 1, n_ep)).wait_recv()

    def ag_all(zb, piece, act_fn, up, down):
        block = zb * INNER + yi
        if up:
            @pl.when(zi < outer - 1)
            def _():
                act_fn(ag_copy(block, 0, piece, me + INNER))
        if down:
            @pl.when(zi > 0)
            def _():
                act_fn(ag_copy(block, 1, piece, me - INNER))
        for j in range(1, INNER):
            act_fn(ag_copy(block, 1 + j, piece, zi * INNER + lax.rem(yi + j, INNER)))

    def source_of(j):
        return lax.rem(hi_rep + j // 2, halves) * 2 + lax.rem(core + j, 2)

    def xs_copy(block, j):
        target = source_of(j)
        return pltpu.make_async_remote_copy(
            src_ref=xg.at[block, :, pl.ds(pl.multiple_of(target * part, 128), part)],
            dst_ref=xs.at[rep, block],
            send_sem=xs_send.at[j, block], recv_sem=xs_recv.at[rep, block],
            device_id={"rep": target}, device_id_type=MESH,
        )

    def xs_begin(block):
        for j in reversed(range(1, n_rep)):
            xs_copy(block, j).start()

    def act_copy(target):
        return pltpu.make_async_remote_copy(
            src_ref=act_hbm, dst_ref=actg.at[rep],
            send_sem=act_send.at[target], recv_sem=act_recv.at[rep],
            device_id={"rep": target}, device_id_type=MESH,
        )

    def fw_copy(source):
        return pltpu.make_async_remote_copy(
            src_ref=actg.at[source], dst_ref=actg.at[source],
            send_sem=fw_send.at[source], recv_sem=act_recv.at[source],
            device_id={"rep": partner}, device_id_type=MESH,
        )

    def rs_copy(target):
        return pltpu.make_async_remote_copy(
            src_ref=rs.at[rep], dst_ref=rs.at[rep],
            send_sem=rs_send.at[target], recv_sem=rs_recv.at[rep],
            device_id={"rep": target}, device_id_type=MESH,
        )

    def rf_copy(source):
        return pltpu.make_async_remote_copy(
            src_ref=rs.at[source], dst_ref=rs.at[source],
            send_sem=rf_send.at[source], recv_sem=rs_recv.at[source],
            device_id={"rep": partner}, device_id_type=MESH,
        )

    for j in range(1, n_ep):
        rg_copy(j).start()
    load_x.wait()
    for piece in range(PIECES):
        ag_all(zi, piece, begin, True, True)
    xs_begin(me)
    for target in cross + [partner]:
        act_copy(target).start()

    def step(s):
        @pl.when(zi - s >= 0)
        def _():
            for piece in range(PIECES):
                ag_arrived((zi - s) * INNER + yi, piece)
                ag_all(zi - s, piece, begin, True, False)
            xs_begin((zi - s) * INNER + yi)

        @pl.when(zi + s < outer)
        def _():
            for piece in range(PIECES):
                ag_arrived((zi + s) * INNER + yi, piece)
                ag_all(zi + s, piece, begin, False, True)
            xs_begin((zi + s) * INNER + yi)

    def side_arrived(first, count):
        for z in range(count):
            for j in range(1, INNER):
                block = (first + z) * INNER + lax.rem(yi + j, INNER)
                for piece in range(PIECES):
                    ag_arrived(block, piece)
                xs_begin(block)

    def back_copy(target):
        return pltpu.make_async_remote_copy(
            src_ref=yb.at[target], dst_ref=rb.at[me],
            send_sem=back_send.at[target], recv_sem=back_recv.at[me],
            device_id={"ep": target}, device_id_type=MESH,
        )

    def gate_column(dense_rows, e):
        lane_g = lax.broadcasted_iota(jnp.int32, dense_rows.shape, 1)
        mine = (lane_g == e) | (lane_g == e + experts)
        return jnp.sum(jnp.where(mine, dense_rows, 0.0), axis=1, keepdims=True)

    def input_rows(first, count, home):
        chunk = min(GROUP, count * INNER)
        rows = chunk * tok

        @pl.loop(0, count * INNER // chunk)
        def _(g):
            blocks = pl.ds(first * INNER + g * chunk, chunk)
            x = xg[blocks].reshape(rows, model)
            dense_rows = rs[rep, blocks].astype(F32).reshape(rows, width)
            for e in range(loc):
                y = jnp.dot(x, wv[e], preferred_element_type=F32)
                y = y * gate_column(dense_rows, me * loc + e)
                yb[blocks, e] = y.astype(BF16).reshape(chunk, tok, hid)

        for j in range(count * INNER):
            target = first * INNER + j
            if home:
                @pl.when(target != me)
                def _():
                    back_copy(target).start()
            else:
                back_copy(target).start()

    step(1)
    for j in range(1, n_ep):
        source = lax.rem(me + j, n_ep)
        pltpu.make_async_remote_copy(
            src_ref=rs.at[rep, source], dst_ref=rs.at[rep, source],
            send_sem=rg_send.at[j], recv_sem=rg_recv.at[source],
            device_id={"ep": source}, device_id_type=MESH,
        ).wait_recv()
    for target in cross + [partner]:
        rs_copy(target).start()
    near_half = outer // 2
    far = near_half // 2
    upper = zi >= near_half
    home_row = jnp.where(upper, near_half, 0)
    first_far = jnp.where(upper, near_half - far, near_half)
    last_far = jnp.where(upper, 0, near_half + far)
    for s in range(2, near_half + 1):
        step(s)
    load_w.wait()
    side_arrived(home_row, near_half)
    input_rows(home_row, near_half, True)
    own_y = pltpu.make_async_copy(yb.at[me], rb.at[me], lsem.at[5])
    own_y.start()
    for s in range(near_half + 1, outer):
        step(s)
    side_arrived(first_far, far)
    input_rows(first_far, far, False)
    load_a.wait()
    for source in cross:
        rf_copy(source).wait_recv()
        rf_copy(source).start()
        fw_copy(source).wait_recv()
        fw_copy(source).start()
    side_arrived(last_far, far)
    input_rows(last_far, far, False)

    own_x = pltpu.make_async_copy(
        xg.at[:, :, pl.ds(pl.multiple_of(rep * part, 128), part)], xs.at[rep], lsem.at[3]
    )
    own_x.start()

    group = min(GROUP, n_ep)
    rows = group * tok
    lane_r = lax.broadcasted_iota(jnp.int32, (rows, width), 1)
    q_r = lax.broadcasted_iota(jnp.int32, (rows, rows), 0)
    q_c = lax.broadcasted_iota(jnp.int32, (rows, rows), 1)
    before = jnp.where((q_r // tok == q_c // tok) & (q_c < q_r), 1.0, 0.0).astype(BF16)
    slots = group * cap
    p_r = lax.broadcasted_iota(jnp.int32, (rows, slots), 0)
    p_c = lax.broadcasted_iota(jnp.int32, (rows, slots), 1)
    offset = (p_c - (p_r // tok) * cap).astype(F32)
    own_x.wait()

    early = n_ep <= GROUP

    def scale_rows(source, g, place):
        blocks = pl.ds(g * group, group)
        dense_rows = rs[source, blocks].reshape(rows, width).astype(F32)
        named = jnp.where(dense_rows > 0.0, 1.0, 0.0)
        earlier = jnp.dot(before, named.astype(BF16), preferred_element_type=F32)
        for e in range(loc):
            mine = lane_r == me * loc + e
            slot = jnp.sum(jnp.where(mine, earlier, 0.0), axis=1, keepdims=True)
            has = jnp.sum(jnp.where(mine, named, 0.0), axis=1, keepdims=True)
            slot = jnp.where(has > 0.0, slot, -1.0)
            pick = jnp.where((offset == slot) & (offset >= 0.0), 1.0, 0.0).astype(BF16)
            saved = actg[source, e, pl.ds(pl.multiple_of(g * slots, 16), slots), :]
            row = jnp.dot(pick, saved, preferred_element_type=F32)
            at[place, e] = (row * gate_column(dense_rows, me * loc + e)).astype(BF16)

    def products(source, g, place, first):
        x_part = xs[source, pl.ds(g * group, group)].reshape(rows, part)
        for e in range(loc):
            term = lax.dot_general(
                x_part, at[place, e], (((0,), (0,)), ((), ())), preferred_element_type=F32
            )
            acc[e] = term if first else acc[e] + term

    def one_source(source, place):
        if early:
            products(source, 0, place, False)
        else:
            @pl.loop(0, n_ep // group)
            def _(g):
                scale_rows(source, g, 0)
                products(source, g, 0, False)

    def act_arrived(j):
        source = source_of(j)

        @pl.when(lax.rem(j, 2) == 1)
        def _():
            rf_copy(source).wait_recv()
            fw_copy(source).wait_recv()

    if early:
        scale_rows(rep, 0, 0)
        products(rep, 0, 0, True)

        @pl.loop(1, n_rep)
        def _(j):
            act_arrived(j)
            scale_rows(source_of(j), 0, j)
    else:
        acc[...] = jnp.zeros_like(acc)
        one_source(rep, 0)

    pairs = tok * topk
    t_r = lax.broadcasted_iota(jnp.int32, (pairs, tok), 0) // topk
    t_c = lax.broadcasted_iota(jnp.int32, (pairs, tok), 1)
    spread = (t_r == t_c).astype(F32).astype(BF16)
    pair_ids = lax.dot_general(
        spread, ids.astype(F32).astype(BF16), (((1,), (1,)), ((), ())),
        preferred_element_type=F32,
    )
    k_r = lax.rem(lax.broadcasted_iota(jnp.int32, (pairs, topk), 0), topk)
    k_c = lax.broadcasted_iota(jnp.int32, (pairs, topk), 1)
    pair_id = jnp.sum(jnp.where(k_r == k_c, pair_ids, 0.0), axis=1, keepdims=True)
    span = group * loc * tok
    s_r = lax.broadcasted_iota(jnp.int32, (pairs, span), 0) // topk
    s_c = lax.broadcasted_iota(jnp.int32, (pairs, span), 1)
    same_token = s_r == lax.rem(s_c, tok)
    s_e = (s_c // tok).astype(F32)
    chosen = [
        jnp.where(same_token & (s_e + float(g * group * loc) == pair_id), 1.0, 0.0).astype(BF16)
        for g in range(n_ep // group)
    ]

    @pl.loop(1, n_rep)
    def _(j):
        source = source_of(j)
        if not early:
            act_arrived(j)

        @pl.loop(0, n_ep)
        def _(block):
            pltpu.make_async_remote_copy(
                src_ref=xs.at[source, block], dst_ref=xs.at[source, block],
                send_sem=xs_send.at[j, block], recv_sem=xs_recv.at[source, block],
                device_id={"rep": partner}, device_id_type=MESH,
            ).wait_recv()

        one_source(source, j)

    wg_ref[...] = acc[...].astype(wg_ref.dtype)

    own_y.wait()
    for j in range(1, n_ep):
        source = lax.rem(me + j, n_ep)
        pltpu.make_async_remote_copy(
            src_ref=yb.at[source], dst_ref=rb.at[source],
            send_sem=back_send.at[j], recv_sem=back_recv.at[source],
            device_id={"ep": source}, device_id_type=MESH,
        ).wait_recv()
    total = jnp.zeros((pairs, hid), F32)
    for g in range(n_ep // group):
        total += jnp.dot(
            chosen[g],
            rb[g * group : (g + 1) * group].reshape(span, hid),
            preferred_element_type=F32,
        )
    ing_ref[...] = total.astype(ing_ref.dtype)

    for j in range(1, n_ep):
        rg_copy(j).wait_send()
    for piece in range(PIECES):
        ag_all(zi, piece, end_send, True, True)
    for s in range(1, outer):
        @pl.when(zi - s >= 0)
        def _():
            for piece in range(PIECES):
                ag_all(zi - s, piece, end_send, True, False)

        @pl.when(zi + s < outer)
        def _():
            for piece in range(PIECES):
                ag_all(zi + s, piece, end_send, False, True)
    for target in cross + [partner]:
        act_copy(target).wait_send()
        rs_copy(target).wait_send()
    for source in cross:
        fw_copy(source).wait_send()
        rf_copy(source).wait_send()

    @pl.loop(0, n_ep)
    def _(block):
        for j in range(1, n_rep):
            xs_copy(block, j).wait_send()

    for j in range(1, n_ep):
        back_copy(lax.rem(me + j, n_ep)).wait_send()


def finish(in_v, w_v, in_out, w_out, sem):
    loc = w_v.shape[0]
    pairs = [(w_v.at[e], w_out.at[e]) for e in range(loc)] + [(in_v, in_out)]
    stores = [pltpu.make_async_copy(p[0], p[1], sem.at[k]) for k, p in enumerate(pairs)]
    for store in stores:
        store.start()
    for store in stores:
        store.wait()


def shards(out_grad, gate_weights, expert_ids, down_weight, act_cache):
    n_ep, n_rep = lax.axis_size("ep"), lax.axis_size("rep")
    tok, topk = expert_ids.shape
    loc, model, hid = down_weight.shape
    experts = loc * n_ep
    width = pl.cdiv(2 * experts, 128) * 128
    part = model // n_rep
    dma = pltpu.SemaphoreType.DMA
    vmem = pl.BlockSpec(memory_space=pltpu.VMEM)
    hbm = pl.BlockSpec(memory_space=pl.ANY)
    in_grad, weight_grad = pl.pallas_call(
        functools.partial(kernel, n_ep, n_rep),
        out_shape=(
            pltpu.VMEM((tok * topk, hid), BF16),
            pltpu.VMEM((loc, part, hid), BF16),
        ),
        in_specs=[hbm, vmem, vmem, hbm, hbm],
        out_specs=(vmem, vmem),
        scratch_shapes=[
            pltpu.VMEM((n_ep, tok, model), BF16),
            pltpu.VMEM((n_rep, n_ep, tok, part), BF16),
            pltpu.VMEM((n_rep, n_ep, tok, width), BF16),
            pltpu.VMEM((n_rep,) + act_cache.shape, BF16),
            pltpu.VMEM((loc, model, hid), BF16),
            pltpu.VMEM((n_ep, loc, tok, hid), BF16),
            pltpu.VMEM((n_ep, loc, tok, hid), BF16),
            pltpu.VMEM((loc, part, hid), F32),
            pltpu.VMEM((n_rep if n_ep <= GROUP else 1, loc, min(GROUP, n_ep) * tok, hid), BF16),
            dma((6,)), dma((1 + INNER, n_ep, PIECES)), dma((n_ep, PIECES)),
            dma((n_ep,)), dma((n_ep,)),
            dma((n_rep,)), dma((n_rep,)), dma((n_rep,)),
            dma((n_rep,)), dma((n_rep,)), dma((n_rep,)),
            dma((n_rep, n_ep)), dma((n_rep, n_ep)),
            dma((n_ep,)), dma((n_ep,)),
        ],
        compiler_params=pltpu.CompilerParams(
            collective_id=0, has_side_effects=True, vmem_limit_bytes=60 * 1024 * 1024
        ),
    )(out_grad, expert_ids.T, gate_weights.T, down_weight, act_cache)
    in_grad, weight_grad = pl.pallas_call(
        finish,
        out_shape=(
            jax.ShapeDtypeStruct((tok * topk, hid), BF16),
            jax.ShapeDtypeStruct((loc, part, hid), BF16),
        ),
        in_specs=[vmem, vmem],
        out_specs=(hbm, hbm),
        scratch_shapes=[dma((1 + loc,))],
        compiler_params=pltpu.CompilerParams(vmem_limit_bytes=1024 * 1024),
    )(
        pltpu.with_memory_space_constraint(in_grad, pltpu.VMEM),
        pltpu.with_memory_space_constraint(weight_grad, pltpu.VMEM),
    )
    return in_grad.reshape(tok, topk, hid), weight_grad


def solution(mesh):
    in_specs = (
        P(("ep", "rep"), None),
        P(("ep", "rep"), None),
        P(("ep", "rep"), None),
        P("ep", None, None),
        P("ep", "rep", None),
    )
    out_specs = (P(("ep", "rep"), None, None), P("ep", "rep", None))
    return jax.shard_map(shards, mesh=mesh, in_specs=in_specs, out_specs=out_specs, check_vma=False)
```

```python
import functools
import jax
import jax.numpy as jnp
from jax import lax
from jax.experimental import pallas as pl
from jax.experimental.pallas import tpu as pltpu
from jax.sharding import PartitionSpec as P

MESH = pl.DeviceIdType.MESH
F32 = jnp.float32
BF16 = jnp.bfloat16
INNER = 2
PIECES = 2
GROUP = 8
LANES = 128
EXT_STEP = 2


def transposed_dot(a, b):
    return lax.dot_general(a, b, (((0,), (0,)), ((), ())), preferred_element_type=F32)


def kernel(
    n_ep, n_rep, ext, pieces, og_hbm, ids_ref, gate_ref, w_hbm, act_hbm, ing_ref, wg_ref,
    xg, xe, xs, dg, gg, gs, actg, wv, yb, rb, acc, at,
    lsem, ag_send, ag_recv, ext_send, ext_recv, xe_send, xe_recv, rg_send, rg_recv,
    act_send, act_recv, fw_send, gs_send, gs_recv, xs_send, xs_recv, back_send, back_recv,
):
    topk, tok = ids_ref.shape
    model = og_hbm.shape[1]
    loc, _, hid = w_hbm.shape
    part = xs.shape[3]
    cap = act_hbm.shape[1] // n_ep
    outer = n_ep // INNER
    half = model // pieces
    sub = dg.shape[1]
    per = LANES // tok
    me = lax.axis_index("ep")
    rep = lax.axis_index("rep")
    zi, yi = me // INNER, lax.rem(me, INNER)
    hi_rep, core = rep // 2, lax.rem(rep, 2)
    halves = n_rep // 2
    cross = [lax.rem(hi_rep + j, halves) * 2 + core for j in range(1, halves)]
    partner = hi_rep * 2 + 1 - core
    early = n_ep <= GROUP

    barrier = pltpu.get_barrier_semaphore()
    for j in range(1, n_ep):
        pl.semaphore_signal(
            barrier, inc=1, device_id={"ep": lax.rem(me + j, n_ep)}, device_id_type=MESH
        )
    for j in range(1, n_rep):
        pl.semaphore_signal(
            barrier, inc=1, device_id={"rep": lax.rem(rep + j, n_rep)}, device_id_type=MESH
        )

    load_x = pltpu.make_async_copy(og_hbm, xg.at[me], lsem.at[0])
    load_x.start()
    load_a = pltpu.make_async_copy(act_hbm, actg.at[rep], lsem.at[1])
    load_a.start()
    load_w = pltpu.make_async_copy(w_hbm, wv, lsem.at[2])
    load_w.start()

    pl.semaphore_wait(barrier, n_ep - 1 + n_rep - 1)

    def begin(copy):
        copy.start()

    def end_send(copy):
        copy.wait_send()

    def rg_copy(j):
        target = lax.rem(me + j, n_ep)
        return pltpu.make_async_remote_copy(
            src_ref=dg.at[target], dst_ref=gg.at[me],
            send_sem=rg_send.at[j], recv_sem=rg_recv.at[me],
            device_id={"ep": target}, device_id_type=MESH,
        )

    def ag_copy(block, way, piece, target):
        cols = pl.ds(piece * half, half)
        return pltpu.make_async_remote_copy(
            src_ref=xg.at[block, :, cols], dst_ref=xg.at[block, :, cols],
            send_sem=ag_send.at[way, block, piece], recv_sem=ag_recv.at[block, piece],
            device_id={"ep": target}, device_id_type=MESH,
        )

    def own_copy(way, piece, target):
        cols = pl.ds(piece * half, half)
        return pltpu.make_async_remote_copy(
            src_ref=og_hbm.at[:, cols], dst_ref=xg.at[me, :, cols],
            send_sem=ag_send.at[way, me, piece], recv_sem=ag_recv.at[me, piece],
            device_id={"ep": target}, device_id_type=MESH,
        )

    def xe_copy(j):
        return pltpu.make_async_remote_copy(
            src_ref=xe.at[me], dst_ref=xe.at[me],
            send_sem=xe_send.at[j], recv_sem=xe_recv.at[me],
            device_id={"ep": lax.rem(me + j, n_ep)}, device_id_type=MESH,
        )

    def xe_arrived(block):
        pltpu.make_async_remote_copy(
            src_ref=xe.at[block], dst_ref=xe.at[block],
            send_sem=xe_send.at[0], recv_sem=xe_recv.at[block],
            device_id={"ep": lax.rem(me + 1, n_ep)}, device_id_type=MESH,
        ).wait_recv()

    def ag_arrived(block, piece):
        ag_copy(block, 0, piece, lax.rem(me + 1, n_ep)).wait_recv()

    def ways(act_fn, copy_of, up, down):
        if up:
            @pl.when(zi < outer - 1)
            def _():
                act_fn(copy_of(0, me + INNER))
        if down:
            @pl.when(zi > 0)
            def _():
                act_fn(copy_of(1, me - INNER))
        for j in range(1, INNER):
            act_fn(copy_of(1 + j, zi * INNER + lax.rem(yi + j, INNER)))

    def ag_own(piece, act_fn):
        ways(act_fn, lambda way, target: own_copy(way, piece, target), True, True)

    def ag_all(zb, piece, act_fn, up, down):
        block = zb * INNER + yi
        ways(act_fn, lambda way, target: ag_copy(block, way, piece, target), up, down)

    def source_of(j):
        return lax.rem(hi_rep + j // 2, halves) * 2 + lax.rem(core + j, 2)

    def ext_copy(k):
        target = lax.rem(hi_rep + 1, halves) * 2 + k
        return pltpu.make_async_remote_copy(
            src_ref=og_hbm.at[:, pl.ds(pl.multiple_of(target * part, LANES), ext)],
            dst_ref=xe.at[me, :, pl.ds(pl.multiple_of(core * ext, LANES), ext)],
            send_sem=ext_send.at[k], recv_sem=ext_recv.at[core],
            device_id={"rep": target}, device_id_type=MESH,
        )

    def ext_arrived(k):
        pltpu.make_async_remote_copy(
            src_ref=og_hbm.at[:, pl.ds(0, ext)],
            dst_ref=xe.at[me, :, pl.ds(k * ext, ext)],
            send_sem=ext_send.at[k], recv_sem=ext_recv.at[k],
            device_id={"rep": partner}, device_id_type=MESH,
        ).wait_recv()

    def xs_copy(block, j, own=False):
        target = source_of(j)
        skip = ext if j > 1 else 0
        cols = pl.ds(pl.multiple_of(target * part + skip, LANES), part - skip)
        return pltpu.make_async_remote_copy(
            src_ref=og_hbm.at[:, cols] if own else xg.at[block, :, cols],
            dst_ref=xs.at[rep, block, :, pl.ds(skip, part - skip)],
            send_sem=xs_send.at[j, block], recv_sem=xs_recv.at[rep, block],
            device_id={"rep": target}, device_id_type=MESH,
        )

    def xs_arrived(j, block):
        source = source_of(j)
        skip = ext if j > 1 else 0
        ref = xs.at[source, block, :, pl.ds(skip, part - skip)]
        pltpu.make_async_remote_copy(
            src_ref=ref, dst_ref=ref,
            send_sem=xs_send.at[j, block], recv_sem=xs_recv.at[source, block],
            device_id={"rep": partner}, device_id_type=MESH,
        ).wait_recv()

    def xs_begin(block, piece):
        for j in reversed(range(1, n_rep)):
            @pl.when(source_of(j) // (n_rep // pieces) == piece)
            def _():
                xs_copy(block, j).start()

    def act_copy(target):
        return pltpu.make_async_remote_copy(
            src_ref=act_hbm, dst_ref=actg.at[rep],
            send_sem=act_send.at[target], recv_sem=act_recv.at[rep],
            device_id={"rep": target}, device_id_type=MESH,
        )

    def fw_copy(source):
        return pltpu.make_async_remote_copy(
            src_ref=actg.at[source], dst_ref=actg.at[source],
            send_sem=fw_send.at[source], recv_sem=act_recv.at[source],
            device_id={"rep": partner}, device_id_type=MESH,
        )

    def gs_copy(j):
        return pltpu.make_async_remote_copy(
            src_ref=gs.at[rep], dst_ref=gs.at[rep],
            send_sem=gs_send.at[j], recv_sem=gs_recv.at[rep],
            device_id={"rep": source_of(j)}, device_id_type=MESH,
        )

    if ext:
        for k in range(2):
            ext_copy(k).start()
    ag_own(0, begin)
    for target in cross:
        act_copy(target).start()
    for piece in range(1, pieces):
        ag_own(piece, begin)
    for j in reversed(range(1, n_rep)):
        xs_copy(me, j, True).start()
    act_copy(partner).start()

    place_r = lax.broadcasted_iota(jnp.int32, (tok, LANES), 0)
    place_c = lax.broadcasted_iota(jnp.int32, (tok, LANES), 1)
    lane_of = jnp.where(place_c == place_r + lax.rem(me, per) * tok, 1.0, 0.0).astype(BF16)
    ids = ids_ref[...].astype(F32)
    gates = gate_ref[...]
    named_by = jnp.dot((ids + 1.0).astype(BF16), lane_of, preferred_element_type=F32)
    gate_by = jnp.dot(gates.astype(BF16), lane_of, preferred_element_type=F32)
    row = lax.broadcasted_iota(jnp.int32, (n_ep * sub, LANES), 0)
    line = jnp.where(lax.rem(row, sub) < loc, row // sub * loc + lax.rem(row, sub) + 1, -1)
    line = line.astype(F32)
    dense = jnp.zeros((n_ep * sub, LANES), F32)
    for k in range(topk):
        dense = jnp.where(line == named_by[k : k + 1, :], gate_by[k : k + 1, :], dense)
    dg[...] = dense.reshape(n_ep, sub, LANES)
    gg[me] = dg[me]
    for j in range(1, n_ep):
        rg_copy(j).start()

    def inside(z):
        return (z >= 0) & (z < outer)

    def lines(s):
        for piece in range(pieces):
            for way in (-1, 1):
                z = zi + way * s

                @pl.when(inside(z))
                def _():
                    ag_arrived(z * INNER + yi, piece)
                    ag_all(z, piece, begin, way < 0, way > 0)
                    xs_begin(z * INNER + yi, piece)

    def sides(z):
        for j in range(1, INNER):
            block = z * INNER + lax.rem(yi + j, INNER)
            for piece in range(pieces):
                ag_arrived(block, piece)
                xs_begin(block, piece)

    def back_copy(target):
        return pltpu.make_async_remote_copy(
            src_ref=yb.at[target], dst_ref=rb.at[me],
            send_sem=back_send.at[target], recv_sem=back_recv.at[me],
            device_id={"ep": target}, device_id_type=MESH,
        )

    def input_rows(s):
        side = lax.rem(yi + 1, INNER)
        first = s == 1
        slots = [
            (jnp.where(first, me, (zi - s + 1) * INNER + side), inside(zi - s + 1)),
            ((zi + s - 1) * INNER + side, inside(zi + s - 1)),
            ((zi - s) * INNER + yi, inside(zi - s)),
            ((zi + s) * INNER + yi, inside(zi + s)),
        ]
        some = functools.reduce(lambda a, b: a | b, [slot[1] for slot in slots])

        @pl.when(some)
        def _():
            any_block = slots[3][0]
            for block, valid in reversed(slots[:3]):
                any_block = jnp.where(valid, block, any_block)
            blocks = [jnp.where(valid, block, any_block) for block, valid in slots]
            x = jnp.concatenate([xg[block] for block in blocks], axis=0)
            for e in range(loc):
                y = jnp.dot(x, wv[e], preferred_element_type=F32).astype(BF16)
                for k, block in enumerate(blocks):
                    yb[block, e] = y[k * tok : (k + 1) * tok]
            for block, valid in slots:
                @pl.when(valid & (block != me))
                def _():
                    back_copy(block).start()

    group = min(GROUP, n_ep)
    tiles = group // per
    slots = per * cap
    b_r = lax.broadcasted_iota(jnp.int32, (LANES, LANES), 0)
    b_c = lax.broadcasted_iota(jnp.int32, (LANES, LANES), 1)
    before = jnp.where((b_r // tok == b_c // tok) & (b_r < b_c), 1.0, 0.0).astype(BF16)
    p_r = lax.broadcasted_iota(jnp.int32, (slots, LANES), 0)
    p_c = lax.broadcasted_iota(jnp.int32, (slots, LANES), 1)
    offset = (p_r - p_c // tok * cap).astype(F32)

    def scale_rows(source, g, place):
        for q in range(tiles):
            gate = gs[source, g * tiles + q]
            named = jnp.where(gate > 0.0, 1.0, 0.0)
            slot = jnp.dot(named.astype(BF16), before, preferred_element_type=F32)
            for e in range(loc):
                pick = jnp.where(offset == slot[e : e + 1, :], gate[e : e + 1, :], 0.0)
                start = pl.multiple_of((g * tiles + q) * slots, 16)
                saved = actg[source, e, pl.ds(start, slots), :]
                at[place, e, pl.ds(q * LANES, LANES)] = transposed_dot(
                    pick.astype(BF16), saved
                ).astype(BF16)

    @pl.loop(1, outer + 1)
    def _(s):
        lines(s)

        @pl.when(s == 1)
        def _():
            for j in range(1, n_ep):
                source = lax.rem(me + j, n_ep)
                pltpu.make_async_remote_copy(
                    src_ref=gg.at[source], dst_ref=gg.at[source],
                    send_sem=rg_send.at[j], recv_sem=rg_recv.at[source],
                    device_id={"ep": source}, device_id_type=MESH,
                ).wait_recv()
            gs[rep] = jnp.sum(gg[...].reshape(n_ep // per, per, sub, LANES), axis=1)
            for j in range(1, n_rep):
                gs_copy(j).start()
            load_x.wait()
            load_w.wait()
            sides(zi)

        @pl.when(s > 1)
        def _():
            for way in (-1, 1):
                z = zi + way * (s - 1)

                @pl.when(inside(z))
                def _():
                    sides(z)

        input_rows(s)

        if ext:
            @pl.when(s == EXT_STEP)
            def _():
                for k in range(2):
                    ext_arrived(k)
                for j in range(1, n_ep):
                    xe_copy(j).start()

    own_y = pltpu.make_async_copy(yb.at[me], rb.at[me], lsem.at[3])
    own_y.start()
    load_a.wait()
    if early:
        scale_rows(rep, 0, 0)

    def act_arrived(source):
        fw_copy(source).wait_recv()

    def gs_arrived(j):
        source = source_of(j)
        pltpu.make_async_remote_copy(
            src_ref=gs.at[source], dst_ref=gs.at[source],
            send_sem=gs_send.at[j], recv_sem=gs_recv.at[source],
            device_id={"rep": source}, device_id_type=MESH,
        ).wait_recv()

    for source in cross:
        act_arrived(source)
        fw_copy(source).start()

    act_arrived(partner)
    for j in range(1, n_rep):
        gs_arrived(j)

    def x_own(g):
        cols = pl.ds(pl.multiple_of(rep * part, LANES), part)
        return xg[pl.ds(g * group, group), :, cols].reshape(group * tok, part)

    def x_near(source, g):
        return xs[source, pl.ds(g * group, group)].reshape(group * tok, part)

    def x_late(source):
        return xs[source, :, :, pl.ds(ext, part - ext)].reshape(n_ep * tok, part - ext)

    def x_ext(source):
        cols = pl.ds(pl.multiple_of(lax.rem(source, 2) * ext, LANES), ext)
        return xe[:, :, cols].reshape(n_ep * tok, ext)

    def wait_blocks(j):
        @pl.loop(0, n_ep)
        def _(block):
            xs_arrived(j, block)

    pairs = tok * topk
    t_r = lax.broadcasted_iota(jnp.int32, (pairs, tok), 0) // topk
    t_c = lax.broadcasted_iota(jnp.int32, (pairs, tok), 1)
    spread = jnp.where(t_r == t_c, 1.0, 0.0).astype(BF16)
    k_r = lax.rem(lax.broadcasted_iota(jnp.int32, (pairs, topk), 0), topk)
    k_c = lax.broadcasted_iota(jnp.int32, (pairs, topk), 1)

    def pair_column(values):
        rows = lax.dot_general(
            spread, values.astype(BF16), (((1,), (1,)), ((), ())), preferred_element_type=F32
        )
        return jnp.sum(jnp.where(k_r == k_c, rows, 0.0), axis=1, keepdims=True)

    span = group * loc * tok
    s_r = lax.broadcasted_iota(jnp.int32, (pairs, span), 0) // topk
    s_c = lax.broadcasted_iota(jnp.int32, (pairs, span), 1)
    same_token = s_r == lax.rem(s_c, tok)
    s_e = (s_c // tok).astype(F32)

    def choose():
        pair_id = pair_column(ids)
        high = gates.astype(BF16).astype(F32)
        pair_gate = pair_column(high) + pair_column(gates - high)
        chosen = [
            jnp.where(same_token & (s_e + float(g * group * loc) == pair_id), 1.0, 0.0).astype(BF16)
            for g in range(n_ep // group)
        ]
        return pair_gate, chosen

    if early:
        for e in range(loc):
            acc[e] = transposed_dot(x_own(0), at[0, e])
        scale_rows(partner, 0, 1)
        wait_blocks(1)
        for e in range(loc):
            acc[e] += transposed_dot(x_near(partner, 0), at[1, e])
        for j in range(2, n_rep):
            if j % 2:
                act_arrived(source_of(j))
            scale_rows(source_of(j), 0, j)
        pair_gate, chosen = choose()
        if ext:
            for j in range(1, n_ep):
                xe_arrived(lax.rem(me + j, n_ep))
            for e in range(loc):
                term = acc[e, pl.ds(0, ext)]
                for j in range(2, n_rep):
                    term += transposed_dot(x_ext(source_of(j)), at[j, e])
                wg_ref[e, pl.ds(0, ext)] = term.astype(BF16)
        for j in range(2, n_rep):
            wait_blocks(j)
            for e in range(loc):
                term = transposed_dot(x_late(source_of(j)), at[j, e])
                total = acc[e, pl.ds(ext, part - ext)] + term
                if j == n_rep - 1:
                    wg_ref[e, pl.ds(ext, part - ext)] = total.astype(BF16)
                else:
                    acc[e, pl.ds(ext, part - ext)] = total
    else:
        acc[...] = jnp.zeros_like(acc)

        @pl.loop(0, n_ep // group)
        def _(g):
            scale_rows(rep, g, 0)
            for e in range(loc):
                acc[e] += transposed_dot(x_own(g), at[0, e])

        @pl.loop(1, n_rep)
        def _(j):
            source = source_of(j)

            @pl.when((j > 1) & (lax.rem(j, 2) == 1))
            def _():
                act_arrived(source)

            @pl.loop(0, n_ep)
            def _(block):
                pltpu.make_async_remote_copy(
                    src_ref=xs.at[source, block], dst_ref=xs.at[source, block],
                    send_sem=xs_send.at[j, block], recv_sem=xs_recv.at[source, block],
                    device_id={"rep": partner}, device_id_type=MESH,
                ).wait_recv()

            @pl.loop(0, n_ep // group)
            def _(g):
                scale_rows(source, g, 0)
                for e in range(loc):
                    acc[e] += transposed_dot(x_near(source, g), at[0, e])

        wg_ref[...] = acc[...].astype(BF16)
        pair_gate, chosen = choose()

    own_y.wait()
    for j in range(1, n_ep):
        source = lax.rem(me + j, n_ep)
        pltpu.make_async_remote_copy(
            src_ref=yb.at[source], dst_ref=rb.at[source],
            send_sem=back_send.at[j], recv_sem=back_recv.at[source],
            device_id={"ep": source}, device_id_type=MESH,
        ).wait_recv()
    total = jnp.zeros((pairs, hid), F32)
    for g in range(n_ep // group):
        total += jnp.dot(
            chosen[g],
            rb[g * group : (g + 1) * group].reshape(span, hid),
            preferred_element_type=F32,
        )
    ing_ref[...] = (total * pair_gate).astype(ing_ref.dtype)

    for j in range(1, n_ep):
        rg_copy(j).wait_send()
    if ext:
        for k in range(2):
            ext_copy(k).wait_send()
        for j in range(1, n_ep):
            xe_copy(j).wait_send()
    for piece in range(pieces):
        ag_own(piece, end_send)
    for s in range(1, outer):
        @pl.when(zi - s >= 0)
        def _():
            for piece in range(pieces):
                ag_all(zi - s, piece, end_send, True, False)

        @pl.when(zi + s < outer)
        def _():
            for piece in range(pieces):
                ag_all(zi + s, piece, end_send, False, True)
    for target in cross + [partner]:
        act_copy(target).wait_send()
    for j in range(1, n_rep):
        gs_copy(j).wait_send()
    for source in cross:
        fw_copy(source).wait_send()

    @pl.loop(0, n_ep)
    def _(block):
        for j in range(1, n_rep):
            xs_copy(block, j).wait_send()

    for j in range(1, n_ep):
        back_copy(lax.rem(me + j, n_ep)).wait_send()


def finish(in_v, w_v, in_out, w_out, sem):
    loc = w_v.shape[0]
    pairs = [(w_v.at[e], w_out.at[e]) for e in range(loc)] + [(in_v, in_out)]
    stores = [pltpu.make_async_copy(p[0], p[1], sem.at[k]) for k, p in enumerate(pairs)]
    for store in stores:
        store.start()
    for store in stores:
        store.wait()


def shards(out_grad, gate_weights, expert_ids, down_weight, act_cache):
    n_ep, n_rep = lax.axis_size("ep"), lax.axis_size("rep")
    tok, topk = expert_ids.shape
    loc, model, hid = down_weight.shape
    part = model // n_rep
    early = n_ep <= GROUP
    pieces = PIECES if early else 1
    ext = part // (4 * LANES) * LANES if n_rep == 4 and early else 0
    sub = pl.cdiv(loc, 8) * 8
    per = LANES // tok
    dma = pltpu.SemaphoreType.DMA
    vmem = pl.BlockSpec(memory_space=pltpu.VMEM)
    hbm = pl.BlockSpec(memory_space=pl.ANY)
    in_grad, weight_grad = pl.pallas_call(
        functools.partial(kernel, n_ep, n_rep, ext, pieces),
        out_shape=(
            pltpu.VMEM((tok * topk, hid), BF16),
            pltpu.VMEM((loc, part, hid), BF16),
        ),
        in_specs=[hbm, vmem, vmem, hbm, hbm],
        out_specs=(vmem, vmem),
        scratch_shapes=[
            pltpu.VMEM((n_ep, tok, model), BF16),
            pltpu.VMEM((n_ep, tok, max(2 * ext, LANES)), BF16),
            pltpu.VMEM((n_rep, n_ep, tok, part), BF16),
            pltpu.VMEM((n_ep, sub, LANES), F32),
            pltpu.VMEM((n_ep, sub, LANES), F32),
            pltpu.VMEM((n_rep, n_ep // per, sub, LANES), F32),
            pltpu.VMEM((n_rep,) + act_cache.shape, BF16),
            pltpu.VMEM((loc, model, hid), BF16),
            pltpu.VMEM((n_ep, loc, tok, hid), BF16),
            pltpu.VMEM((n_ep, loc, tok, hid), BF16),
            pltpu.VMEM((loc, part, hid), F32),
            pltpu.VMEM((n_rep if early else 1, loc, min(GROUP, n_ep) * tok, hid), BF16),
            dma((4,)), dma((1 + INNER, n_ep, pieces)), dma((n_ep, pieces)),
            dma((2,)), dma((2,)), dma((n_ep,)), dma((n_ep,)),
            dma((n_ep,)), dma((n_ep,)),
            dma((n_rep,)), dma((n_rep,)), dma((n_rep,)),
            dma((n_rep,)), dma((n_rep,)),
            dma((n_rep, n_ep)), dma((n_rep, n_ep)),
            dma((n_ep,)), dma((n_ep,)),
        ],
        compiler_params=pltpu.CompilerParams(
            collective_id=0, has_side_effects=True, vmem_limit_bytes=60 * 1024 * 1024
        ),
    )(out_grad, expert_ids.T, gate_weights.T, down_weight, act_cache)
    in_grad, weight_grad = pl.pallas_call(
        finish,
        out_shape=(
            jax.ShapeDtypeStruct((tok * topk, hid), BF16),
            jax.ShapeDtypeStruct((loc, part, hid), BF16),
        ),
        in_specs=[vmem, vmem],
        out_specs=(hbm, hbm),
        scratch_shapes=[dma((1 + loc,))],
        compiler_params=pltpu.CompilerParams(vmem_limit_bytes=1024 * 1024),
    )(
        pltpu.with_memory_space_constraint(in_grad, pltpu.VMEM),
        pltpu.with_memory_space_constraint(weight_grad, pltpu.VMEM),
    )
    return in_grad.reshape(tok, topk, hid), weight_grad


def solution(mesh):
    in_specs = (
        P(("ep", "rep"), None),
        P(("ep", "rep"), None),
        P(("ep", "rep"), None),
        P("ep", None, None),
        P("ep", "rep", None),
    )
    out_specs = (P(("ep", "rep"), None, None), P("ep", "rep", None))
    return jax.shard_map(shards, mesh=mesh, in_specs=in_specs, out_specs=out_specs, check_vma=False)
```

```python
import functools
import jax
import jax.numpy as jnp
from jax import lax
from jax.experimental import pallas as pl
from jax.experimental.pallas import tpu as pltpu
from jax.sharding import PartitionSpec as P

MESH = pl.DeviceIdType.MESH
F32 = jnp.float32
BF16 = jnp.bfloat16
INNER = 2
PIECES = 2
GROUP = 8
LANES = 128
EXT_STEP = 2


def transposed_dot(a, b):
    return lax.dot_general(a, b, (((0,), (0,)), ((), ())), preferred_element_type=F32)


def kernel(
    n_ep, n_rep, ext, pieces, og_hbm, ids_ref, gate_ref, w_hbm, act_hbm, ing_ref, wg_ref,
    xg, xe, xs, dg, gg, gs, actg, wv, yb, rb, acc, at, chosen, pair_gate,
    lsem, ag_send, ag_recv, ext_send, ext_recv, xe_send, xe_recv, rg_send, rg_recv,
    act_send, act_recv, fw_send, gs_send, gs_recv, xs_send, xs_recv, back_send, back_recv,
):
    topk, tok = ids_ref.shape
    model = og_hbm.shape[1]
    loc, _, hid = w_hbm.shape
    part = xs.shape[3]
    cap = act_hbm.shape[1] // n_ep
    outer = n_ep // INNER
    half = model // pieces
    sub = dg.shape[1]
    per = LANES // tok
    me = lax.axis_index("ep")
    rep = lax.axis_index("rep")
    zi, yi = me // INNER, lax.rem(me, INNER)
    hi_rep, core = rep // 2, lax.rem(rep, 2)
    halves = n_rep // 2
    cross = [lax.rem(hi_rep + j, halves) * 2 + core for j in range(1, halves)]
    partner = hi_rep * 2 + 1 - core
    early = n_ep <= GROUP
    helped = core == 1

    barrier = pltpu.get_barrier_semaphore()
    for j in range(1, n_ep):
        pl.semaphore_signal(
            barrier, inc=1, device_id={"ep": lax.rem(me + j, n_ep)}, device_id_type=MESH
        )
    for j in range(1, n_rep):
        pl.semaphore_signal(
            barrier, inc=1, device_id={"rep": lax.rem(rep + j, n_rep)}, device_id_type=MESH
        )

    load_x = pltpu.make_async_copy(og_hbm, xg.at[me], lsem.at[0])
    load_x.start()
    load_a = pltpu.make_async_copy(act_hbm, actg.at[rep], lsem.at[1])
    load_a.start()
    load_w = pltpu.make_async_copy(w_hbm, wv, lsem.at[2])
    load_w.start()

    pl.semaphore_wait(barrier, n_ep - 1 + n_rep - 1)

    def begin(copy):
        copy.start()

    def end_send(copy):
        copy.wait_send()

    def rg_copy(j):
        target = lax.rem(me + j, n_ep)
        return pltpu.make_async_remote_copy(
            src_ref=dg.at[target], dst_ref=gg.at[me],
            send_sem=rg_send.at[j], recv_sem=rg_recv.at[me],
            device_id={"ep": target}, device_id_type=MESH,
        )

    def ag_copy(block, way, piece, target):
        cols = pl.ds(piece * half, half)
        return pltpu.make_async_remote_copy(
            src_ref=xg.at[block, :, cols], dst_ref=xg.at[block, :, cols],
            send_sem=ag_send.at[way, block, piece], recv_sem=ag_recv.at[block, piece],
            device_id={"ep": target}, device_id_type=MESH,
        )

    def own_copy(way, piece, target):
        cols = pl.ds(piece * half, half)
        return pltpu.make_async_remote_copy(
            src_ref=og_hbm.at[:, cols], dst_ref=xg.at[me, :, cols],
            send_sem=ag_send.at[way, me, piece], recv_sem=ag_recv.at[me, piece],
            device_id={"ep": target}, device_id_type=MESH,
        )

    def xe_copy(j):
        return pltpu.make_async_remote_copy(
            src_ref=xe.at[me], dst_ref=xe.at[me],
            send_sem=xe_send.at[j], recv_sem=xe_recv.at[me],
            device_id={"ep": lax.rem(me + j, n_ep)}, device_id_type=MESH,
        )

    def xe_arrived(block):
        pltpu.make_async_remote_copy(
            src_ref=xe.at[block], dst_ref=xe.at[block],
            send_sem=xe_send.at[0], recv_sem=xe_recv.at[block],
            device_id={"ep": lax.rem(me + 1, n_ep)}, device_id_type=MESH,
        ).wait_recv()

    def ag_arrived(block, piece):
        ag_copy(block, 0, piece, lax.rem(me + 1, n_ep)).wait_recv()

    def ways(act_fn, copy_of, up, down):
        if up:
            @pl.when(zi < outer - 1)
            def _():
                act_fn(copy_of(0, me + INNER))
        if down:
            @pl.when(zi > 0)
            def _():
                act_fn(copy_of(1, me - INNER))
        for j in range(1, INNER):
            act_fn(copy_of(1 + j, zi * INNER + lax.rem(yi + j, INNER)))

    def ag_own(piece, act_fn):
        ways(act_fn, lambda way, target: own_copy(way, piece, target), True, True)

    def ag_all(zb, piece, act_fn, up, down):
        block = zb * INNER + yi
        ways(act_fn, lambda way, target: ag_copy(block, way, piece, target), up, down)

    def source_of(j):
        return lax.rem(hi_rep + j // 2, halves) * 2 + lax.rem(core + j, 2)

    def ext_copy(k):
        target = lax.rem(hi_rep + 1, halves) * 2 + k
        return pltpu.make_async_remote_copy(
            src_ref=og_hbm.at[:, pl.ds(pl.multiple_of(target * part, LANES), ext)],
            dst_ref=xe.at[me, :, pl.ds(pl.multiple_of(core * ext, LANES), ext)],
            send_sem=ext_send.at[k], recv_sem=ext_recv.at[core],
            device_id={"rep": target}, device_id_type=MESH,
        )

    def ext_arrived(k):
        pltpu.make_async_remote_copy(
            src_ref=og_hbm.at[:, pl.ds(0, ext)],
            dst_ref=xe.at[me, :, pl.ds(k * ext, ext)],
            send_sem=ext_send.at[k], recv_sem=ext_recv.at[k],
            device_id={"rep": partner}, device_id_type=MESH,
        ).wait_recv()

    def xs_copy(block, j, own=False, skip=0):
        target = source_of(j)
        cols = pl.ds(pl.multiple_of(target * part + skip, LANES), part - skip)
        return pltpu.make_async_remote_copy(
            src_ref=og_hbm.at[:, cols] if own else xg.at[block, :, cols],
            dst_ref=xs.at[rep, block, :, pl.ds(skip, part - skip)],
            send_sem=xs_send.at[j, block], recv_sem=xs_recv.at[rep, block],
            device_id={"rep": target}, device_id_type=MESH,
        )

    def xs_each(act_fn, block, j, own=False):
        if ext and j > 1:
            to_helped = lax.rem(source_of(j), 2) == 1
            for here, skip in ((to_helped, ext), (~to_helped, 0)):
                @pl.when(here)
                def _():
                    act_fn(xs_copy(block, j, own, skip))
        else:
            act_fn(xs_copy(block, j, own))

    def xs_arrived(j, block, skip):
        source = source_of(j)
        ref = xs.at[source, block, :, pl.ds(skip, part - skip)]
        pltpu.make_async_remote_copy(
            src_ref=ref, dst_ref=ref,
            send_sem=xs_send.at[j, block], recv_sem=xs_recv.at[source, block],
            device_id={"rep": partner}, device_id_type=MESH,
        ).wait_recv()

    def xs_begin(block, piece):
        for j in reversed(range(1, n_rep)):
            @pl.when(source_of(j) // (n_rep // pieces) == piece)
            def _():
                xs_each(begin, block, j)

    def act_copy(target):
        return pltpu.make_async_remote_copy(
            src_ref=act_hbm, dst_ref=actg.at[rep],
            send_sem=act_send.at[target], recv_sem=act_recv.at[rep],
            device_id={"rep": target}, device_id_type=MESH,
        )

    def fw_copy(source):
        return pltpu.make_async_remote_copy(
            src_ref=actg.at[source], dst_ref=actg.at[source],
            send_sem=fw_send.at[source], recv_sem=act_recv.at[source],
            device_id={"rep": partner}, device_id_type=MESH,
        )

    def gs_copy(j):
        return pltpu.make_async_remote_copy(
            src_ref=gs.at[rep], dst_ref=gs.at[rep],
            send_sem=gs_send.at[j], recv_sem=gs_recv.at[rep],
            device_id={"rep": source_of(j)}, device_id_type=MESH,
        )

    if ext:
        ext_copy(1).start()
    ag_own(0, begin)
    for target in cross:
        act_copy(target).start()
    for piece in range(1, pieces):
        ag_own(piece, begin)
    for j in reversed(range(1, n_rep)):
        xs_each(begin, me, j, True)
    act_copy(partner).start()

    place_r = lax.broadcasted_iota(jnp.int32, (tok, LANES), 0)
    place_c = lax.broadcasted_iota(jnp.int32, (tok, LANES), 1)
    lane_of = jnp.where(place_c == place_r + lax.rem(me, per) * tok, 1.0, 0.0).astype(BF16)
    ids = ids_ref[...].astype(F32)
    gates = gate_ref[...]
    named_by = jnp.dot((ids + 1.0).astype(BF16), lane_of, preferred_element_type=F32)
    gate_by = jnp.dot(gates.astype(BF16), lane_of, preferred_element_type=F32)
    row = lax.broadcasted_iota(jnp.int32, (n_ep * sub, LANES), 0)
    line = jnp.where(lax.rem(row, sub) < loc, row // sub * loc + lax.rem(row, sub) + 1, -1)
    line = line.astype(F32)
    dense = jnp.zeros((n_ep * sub, LANES), F32)
    for k in range(topk):
        dense = jnp.where(line == named_by[k : k + 1, :], gate_by[k : k + 1, :], dense)
    dg[...] = dense.reshape(n_ep, sub, LANES)
    gg[me] = dg[me]
    for j in range(1, n_ep):
        rg_copy(j).start()

    def inside(z):
        return (z >= 0) & (z < outer)

    def lines(s):
        for piece in range(pieces):
            for way in (-1, 1):
                z = zi + way * s

                @pl.when(inside(z))
                def _():
                    ag_arrived(z * INNER + yi, piece)
                    ag_all(z, piece, begin, way < 0, way > 0)
                    xs_begin(z * INNER + yi, piece)

    def sides(z):
        for j in range(1, INNER):
            block = z * INNER + lax.rem(yi + j, INNER)
            for piece in range(pieces):
                ag_arrived(block, piece)
                xs_begin(block, piece)

    def back_copy(target):
        return pltpu.make_async_remote_copy(
            src_ref=yb.at[target], dst_ref=rb.at[me],
            send_sem=back_send.at[target], recv_sem=back_recv.at[me],
            device_id={"ep": target}, device_id_type=MESH,
        )

    def input_rows(s):
        side = lax.rem(yi + 1, INNER)
        first = s == 1
        slots = [
            (jnp.where(first, me, (zi - s + 1) * INNER + side), inside(zi - s + 1)),
            ((zi + s - 1) * INNER + side, inside(zi + s - 1)),
            ((zi - s) * INNER + yi, inside(zi - s)),
            ((zi + s) * INNER + yi, inside(zi + s)),
        ]
        some = functools.reduce(lambda a, b: a | b, [slot[1] for slot in slots])

        @pl.when(some)
        def _():
            any_block = slots[3][0]
            for block, valid in reversed(slots[:3]):
                any_block = jnp.where(valid, block, any_block)
            blocks = [jnp.where(valid, block, any_block) for block, valid in slots]
            x = jnp.concatenate([xg[block] for block in blocks], axis=0)
            for e in range(loc):
                y = jnp.dot(x, wv[e], preferred_element_type=F32).astype(BF16)
                for k, block in enumerate(blocks):
                    yb[block, e] = y[k * tok : (k + 1) * tok]
            for block, valid in slots:
                @pl.when(valid & (block != me))
                def _():
                    back_copy(block).start()

    group = min(GROUP, n_ep)
    tiles = group // per
    slots = per * cap
    b_r = lax.broadcasted_iota(jnp.int32, (LANES, LANES), 0)
    b_c = lax.broadcasted_iota(jnp.int32, (LANES, LANES), 1)
    before = jnp.where((b_r // tok == b_c // tok) & (b_r < b_c), 1.0, 0.0).astype(BF16)
    p_r = lax.broadcasted_iota(jnp.int32, (slots, LANES), 0)
    p_c = lax.broadcasted_iota(jnp.int32, (slots, LANES), 1)
    offset = (p_r - p_c // tok * cap).astype(F32)

    def scale_rows(source, g, place):
        for q in range(tiles):
            gate = gs[source, g * tiles + q]
            named = jnp.where(gate > 0.0, 1.0, 0.0)
            slot = jnp.dot(named.astype(BF16), before, preferred_element_type=F32)
            for e in range(loc):
                pick = jnp.where(offset == slot[e : e + 1, :], gate[e : e + 1, :], 0.0)
                start = pl.multiple_of((g * tiles + q) * slots, 16)
                saved = actg[source, e, pl.ds(start, slots), :]
                at[place, e, pl.ds(q * LANES, LANES)] = transposed_dot(
                    pick.astype(BF16), saved
                ).astype(BF16)

    def act_arrived(source):
        fw_copy(source).wait_recv()

    def gs_arrived(j):
        source = source_of(j)
        pltpu.make_async_remote_copy(
            src_ref=gs.at[source], dst_ref=gs.at[source],
            send_sem=gs_send.at[j], recv_sem=gs_recv.at[source],
            device_id={"rep": source}, device_id_type=MESH,
        ).wait_recv()

    pairs = tok * topk
    t_r = lax.broadcasted_iota(jnp.int32, (pairs, tok), 0) // topk
    t_c = lax.broadcasted_iota(jnp.int32, (pairs, tok), 1)
    spread = jnp.where(t_r == t_c, 1.0, 0.0).astype(BF16)
    k_r = lax.rem(lax.broadcasted_iota(jnp.int32, (pairs, topk), 0), topk)
    k_c = lax.broadcasted_iota(jnp.int32, (pairs, topk), 1)

    def pair_column(values):
        rows = lax.dot_general(
            spread, values.astype(BF16), (((1,), (1,)), ((), ())), preferred_element_type=F32
        )
        return jnp.sum(jnp.where(k_r == k_c, rows, 0.0), axis=1, keepdims=True)

    span = group * loc * tok
    s_r = lax.broadcasted_iota(jnp.int32, (pairs, span), 0) // topk
    s_c = lax.broadcasted_iota(jnp.int32, (pairs, span), 1)
    same_token = s_r == lax.rem(s_c, tok)
    s_e = (s_c // tok).astype(F32)

    def choose():
        pair_id = pair_column(ids)
        high = gates.astype(BF16).astype(F32)
        pair_gate[...] = pair_column(high) + pair_column(gates - high)
        for g in range(n_ep // group):
            mine = same_token & (s_e + float(g * group * loc) == pair_id)
            chosen[g] = jnp.where(mine, 1.0, 0.0).astype(BF16)

    @pl.loop(1, outer + 1)
    def _(s):
        lines(s)

        @pl.when(s == 1)
        def _():
            for j in range(1, n_ep):
                source = lax.rem(me + j, n_ep)
                pltpu.make_async_remote_copy(
                    src_ref=gg.at[source], dst_ref=gg.at[source],
                    send_sem=rg_send.at[j], recv_sem=rg_recv.at[source],
                    device_id={"ep": source}, device_id_type=MESH,
                ).wait_recv()
            gs[rep] = jnp.sum(gg[...].reshape(n_ep // per, per, sub, LANES), axis=1)
            for j in range(1, n_rep):
                gs_copy(j).start()
            load_x.wait()
            load_w.wait()
            sides(zi)

        @pl.when(s > 1)
        def _():
            for way in (-1, 1):
                z = zi + way * (s - 1)

                @pl.when(inside(z))
                def _():
                    sides(z)

        input_rows(s)

        @pl.when(s == 2)
        def _():
            choose()
            if early:
                load_a.wait()
                scale_rows(rep, 0, 0)
                act_arrived(partner)
                gs_arrived(1)
                scale_rows(partner, 0, 1)

        if ext:
            @pl.when((s == EXT_STEP) & helped)
            def _():
                for k in range(2):
                    ext_arrived(k)
                for j in range(1, n_ep):
                    xe_copy(j).start()

    own_y = pltpu.make_async_copy(yb.at[me], rb.at[me], lsem.at[3])
    own_y.start()
    if not early:
        load_a.wait()

    for source in cross:
        act_arrived(source)
        fw_copy(source).start()

    if not early:
        act_arrived(partner)
        gs_arrived(1)
    for j in range(2, n_rep):
        gs_arrived(j)

    def x_own(g):
        cols = pl.ds(pl.multiple_of(rep * part, LANES), part)
        return xg[pl.ds(g * group, group), :, cols].reshape(group * tok, part)

    def x_near(source, g):
        return xs[source, pl.ds(g * group, group)].reshape(group * tok, part)

    def x_late(first, count, skip):
        return jnp.concatenate([
            xs[source_of(j), pl.ds(first, count), :, pl.ds(skip, part - skip)].reshape(
                count * tok, part - skip
            )
            for j in range(2, n_rep)
        ], axis=0)

    def at_late(e, first, count):
        rows = pl.ds(pl.multiple_of(first * tok, LANES // 2), count * tok)
        return jnp.concatenate([at[j, e, rows, :] for j in range(2, n_rep)], axis=0)

    def x_ext(source):
        cols = pl.ds(pl.multiple_of(lax.rem(source, 2) * ext, LANES), ext)
        return xe[:, :, cols].reshape(n_ep * tok, ext)

    def wait_blocks(j, skip, first=0, count=n_ep):
        @pl.loop(0, count)
        def _(k):
            xs_arrived(j, first + k, skip)

    def far_products(skip):
        if skip:
            for j in range(1, n_ep):
                xe_arrived(lax.rem(me + j, n_ep))
            for e in range(loc):
                term = acc[e, pl.ds(0, skip)]
                for j in range(2, n_rep):
                    term += transposed_dot(x_ext(source_of(j)), at[j, e])
                wg_ref[e, pl.ds(0, skip)] = term.astype(BF16)
        rest = pl.ds(skip, part - skip)
        late = INNER
        soon = jnp.where(zi >= outer // 2, late, 0)
        last = jnp.where(zi >= outer // 2, 0, n_ep - late)
        for first, count in ((soon, n_ep - late), (last, late)):
            for j in range(2, n_rep):
                wait_blocks(j, skip, first, count)
            x_part = x_late(first, count, skip)
            for e in range(loc):
                total = acc[e, rest] + transposed_dot(x_part, at_late(e, first, count))
                if count == late:
                    wg_ref[e, rest] = total.astype(BF16)
                else:
                    acc[e, rest] = total

    if early:
        for e in range(loc):
            acc[e] = transposed_dot(x_own(0), at[0, e])
        wait_blocks(1, 0)
        for e in range(loc):
            acc[e] += transposed_dot(x_near(partner, 0), at[1, e])
        for j in range(2, n_rep):
            if j % 2:
                act_arrived(source_of(j))
            scale_rows(source_of(j), 0, j)
        if ext:
            for here, skip in ((helped, ext), (~helped, 0)):
                @pl.when(here)
                def _():
                    far_products(skip)
        else:
            far_products(0)
    else:
        acc[...] = jnp.zeros_like(acc)

        @pl.loop(0, n_ep // group)
        def _(g):
            scale_rows(rep, g, 0)
            for e in range(loc):
                acc[e] += transposed_dot(x_own(g), at[0, e])

        @pl.loop(1, n_rep)
        def _(j):
            source = source_of(j)

            @pl.when((j > 1) & (lax.rem(j, 2) == 1))
            def _():
                act_arrived(source)

            @pl.loop(0, n_ep)
            def _(block):
                pltpu.make_async_remote_copy(
                    src_ref=xs.at[source, block], dst_ref=xs.at[source, block],
                    send_sem=xs_send.at[j, block], recv_sem=xs_recv.at[source, block],
                    device_id={"rep": partner}, device_id_type=MESH,
                ).wait_recv()

            @pl.loop(0, n_ep // group)
            def _(g):
                scale_rows(source, g, 0)
                for e in range(loc):
                    acc[e] += transposed_dot(x_near(source, g), at[0, e])

        wg_ref[...] = acc[...].astype(BF16)

    own_y.wait()
    for j in range(1, n_ep):
        source = lax.rem(me + j, n_ep)
        pltpu.make_async_remote_copy(
            src_ref=yb.at[source], dst_ref=rb.at[source],
            send_sem=back_send.at[j], recv_sem=back_recv.at[source],
            device_id={"ep": source}, device_id_type=MESH,
        ).wait_recv()
    total = jnp.zeros((pairs, hid), F32)
    for g in range(n_ep // group):
        total += jnp.dot(
            chosen[g],
            rb[g * group : (g + 1) * group].reshape(span, hid),
            preferred_element_type=F32,
        )
    ing_ref[...] = (total * pair_gate[...]).astype(ing_ref.dtype)

    for j in range(1, n_ep):
        rg_copy(j).wait_send()
    if ext:
        ext_copy(1).wait_send()

        @pl.when(helped)
        def _():
            for j in range(1, n_ep):
                xe_copy(j).wait_send()
    for piece in range(pieces):
        ag_own(piece, end_send)
    for s in range(1, outer):
        @pl.when(zi - s >= 0)
        def _():
            for piece in range(pieces):
                ag_all(zi - s, piece, end_send, True, False)

        @pl.when(zi + s < outer)
        def _():
            for piece in range(pieces):
                ag_all(zi + s, piece, end_send, False, True)
    for target in cross + [partner]:
        act_copy(target).wait_send()
    for j in range(1, n_rep):
        gs_copy(j).wait_send()
    for source in cross:
        fw_copy(source).wait_send()

    @pl.loop(0, n_ep)
    def _(block):
        for j in range(1, n_rep):
            xs_each(end_send, block, j)

    for j in range(1, n_ep):
        back_copy(lax.rem(me + j, n_ep)).wait_send()


def finish(in_v, w_v, in_out, w_out, sem):
    loc = w_v.shape[0]
    pairs = [(w_v.at[e], w_out.at[e]) for e in range(loc)] + [(in_v, in_out)]
    stores = [pltpu.make_async_copy(p[0], p[1], sem.at[k]) for k, p in enumerate(pairs)]
    for store in stores:
        store.start()
    for store in stores:
        store.wait()


def shards(out_grad, gate_weights, expert_ids, down_weight, act_cache):
    n_ep, n_rep = lax.axis_size("ep"), lax.axis_size("rep")
    tok, topk = expert_ids.shape
    loc, model, hid = down_weight.shape
    part = model // n_rep
    early = n_ep <= GROUP
    pieces = PIECES if early else 1
    ext = part // (4 * LANES) * LANES if n_rep == 4 and early else 0
    sub = pl.cdiv(loc, 8) * 8
    per = LANES // tok
    dma = pltpu.SemaphoreType.DMA
    vmem = pl.BlockSpec(memory_space=pltpu.VMEM)
    hbm = pl.BlockSpec(memory_space=pl.ANY)
    in_grad, weight_grad = pl.pallas_call(
        functools.partial(kernel, n_ep, n_rep, ext, pieces),
        out_shape=(
            pltpu.VMEM((tok * topk, hid), BF16),
            pltpu.VMEM((loc, part, hid), BF16),
        ),
        in_specs=[hbm, vmem, vmem, hbm, hbm],
        out_specs=(vmem, vmem),
        scratch_shapes=[
            pltpu.VMEM((n_ep, tok, model), BF16),
            pltpu.VMEM((n_ep, tok, max(2 * ext, LANES)), BF16),
            pltpu.VMEM((n_rep, n_ep, tok, part), BF16),
            pltpu.VMEM((n_ep, sub, LANES), F32),
            pltpu.VMEM((n_ep, sub, LANES), F32),
            pltpu.VMEM((n_rep, n_ep // per, sub, LANES), F32),
            pltpu.VMEM((n_rep,) + act_cache.shape, BF16),
            pltpu.VMEM((loc, model, hid), BF16),
            pltpu.VMEM((n_ep, loc, tok, hid), BF16),
            pltpu.VMEM((n_ep, loc, tok, hid), BF16),
            pltpu.VMEM((loc, part, hid), F32),
            pltpu.VMEM((n_rep if early else 1, loc, min(GROUP, n_ep) * tok, hid), BF16),
            pltpu.VMEM((n_ep // min(GROUP, n_ep), tok * topk, min(GROUP, n_ep) * loc * tok), BF16),
            pltpu.VMEM((tok * topk, 1), F32),
            dma((4,)), dma((1 + INNER, n_ep, pieces)), dma((n_ep, pieces)),
            dma((2,)), dma((2,)), dma((n_ep,)), dma((n_ep,)),
            dma((n_ep,)), dma((n_ep,)),
            dma((n_rep,)), dma((n_rep,)), dma((n_rep,)),
            dma((n_rep,)), dma((n_rep,)),
            dma((n_rep, n_ep)), dma((n_rep, n_ep)),
            dma((n_ep,)), dma((n_ep,)),
        ],
        compiler_params=pltpu.CompilerParams(
            collective_id=0, has_side_effects=True, vmem_limit_bytes=60 * 1024 * 1024
        ),
    )(out_grad, expert_ids.T, gate_weights.T, down_weight, act_cache)
    in_grad, weight_grad = pl.pallas_call(
        finish,
        out_shape=(
            jax.ShapeDtypeStruct((tok * topk, hid), BF16),
            jax.ShapeDtypeStruct((loc, part, hid), BF16),
        ),
        in_specs=[vmem, vmem],
        out_specs=(hbm, hbm),
        scratch_shapes=[dma((1 + loc,))],
        compiler_params=pltpu.CompilerParams(vmem_limit_bytes=1024 * 1024),
    )(
        pltpu.with_memory_space_constraint(in_grad, pltpu.VMEM),
        pltpu.with_memory_space_constraint(weight_grad, pltpu.VMEM),
    )
    return in_grad.reshape(tok, topk, hid), weight_grad


def solution(mesh):
    in_specs = (
        P(("ep", "rep"), None),
        P(("ep", "rep"), None),
        P(("ep", "rep"), None),
        P("ep", None, None),
        P("ep", "rep", None),
    )
    out_specs = (P(("ep", "rep"), None, None), P("ep", "rep", None))
    return jax.shard_map(shards, mesh=mesh, in_specs=in_specs, out_specs=out_specs, check_vma=False)
```

```python
import functools
import jax
import jax.numpy as jnp
from jax import lax
from jax.experimental import pallas as pl
from jax.experimental.pallas import tpu as pltpu
from jax.sharding import PartitionSpec as P

MESH = pl.DeviceIdType.MESH
F32 = jnp.float32
BF16 = jnp.bfloat16
INNER = 2
PIECES = 2
GROUP = 8
LANES = 128
EXT_STEP = 2


def transposed_dot(a, b):
    return lax.dot_general(a, b, (((0,), (0,)), ((), ())), preferred_element_type=F32)


def kernel(
    n_ep, n_rep, ext, pieces, og_hbm, ids_ref, gate_ref, w_hbm, act_hbm, ing_ref, wg_ref,
    xg, xe, xs, dg, gg, gs, actg, wv, yb, rb, acc, at, chosen, pair_gate,
    lsem, ag_send, ag_recv, ext_send, ext_recv, xe_send, xe_recv, rg_send, rg_recv,
    act_send, act_recv, fw_send, gs_send, gs_recv, xs_send, xs_recv, back_send, back_recv,
):
    topk, tok = ids_ref.shape
    model = og_hbm.shape[1]
    loc, _, hid = w_hbm.shape
    part = xs.shape[3]
    cap = act_hbm.shape[1] // n_ep
    outer = n_ep // INNER
    half = model // pieces
    sub = dg.shape[1]
    per = LANES // tok
    me = lax.axis_index("ep")
    rep = lax.axis_index("rep")
    zi, yi = me // INNER, lax.rem(me, INNER)
    hi_rep, core = rep // 2, lax.rem(rep, 2)
    halves = n_rep // 2
    cross = [lax.rem(hi_rep + j, halves) * 2 + core for j in range(1, halves)]
    partner = hi_rep * 2 + 1 - core
    early = n_ep <= GROUP
    helped = core == 1

    barrier = pltpu.get_barrier_semaphore()
    for j in range(1, n_ep):
        pl.semaphore_signal(
            barrier, inc=1, device_id={"ep": lax.rem(me + j, n_ep)}, device_id_type=MESH
        )
    for j in range(1, n_rep):
        pl.semaphore_signal(
            barrier, inc=1, device_id={"rep": lax.rem(rep + j, n_rep)}, device_id_type=MESH
        )

    load_x = pltpu.make_async_copy(og_hbm, xg.at[me], lsem.at[0])
    load_x.start()
    load_a = pltpu.make_async_copy(act_hbm, actg.at[rep], lsem.at[1])
    load_a.start()
    load_w = pltpu.make_async_copy(w_hbm, wv, lsem.at[2])
    load_w.start()

    pl.semaphore_wait(barrier, n_ep - 1 + n_rep - 1)

    def begin(copy):
        copy.start()

    def end_send(copy):
        copy.wait_send()

    def rg_copy(j):
        target = lax.rem(me + j, n_ep)
        return pltpu.make_async_remote_copy(
            src_ref=dg.at[target], dst_ref=gg.at[me],
            send_sem=rg_send.at[j], recv_sem=rg_recv.at[me],
            device_id={"ep": target}, device_id_type=MESH,
        )

    def ag_copy(block, way, piece, target):
        cols = pl.ds(piece * half, half)
        return pltpu.make_async_remote_copy(
            src_ref=xg.at[block, :, cols], dst_ref=xg.at[block, :, cols],
            send_sem=ag_send.at[way, block, piece], recv_sem=ag_recv.at[block, piece],
            device_id={"ep": target}, device_id_type=MESH,
        )

    def own_copy(way, piece, target):
        cols = pl.ds(piece * half, half)
        return pltpu.make_async_remote_copy(
            src_ref=og_hbm.at[:, cols], dst_ref=xg.at[me, :, cols],
            send_sem=ag_send.at[way, me, piece], recv_sem=ag_recv.at[me, piece],
            device_id={"ep": target}, device_id_type=MESH,
        )

    def xe_copy(j):
        return pltpu.make_async_remote_copy(
            src_ref=xe.at[me], dst_ref=xe.at[me],
            send_sem=xe_send.at[j], recv_sem=xe_recv.at[me],
            device_id={"ep": lax.rem(me + j, n_ep)}, device_id_type=MESH,
        )

    def xe_arrived(block):
        pltpu.make_async_remote_copy(
            src_ref=xe.at[block], dst_ref=xe.at[block],
            send_sem=xe_send.at[0], recv_sem=xe_recv.at[block],
            device_id={"ep": lax.rem(me + 1, n_ep)}, device_id_type=MESH,
        ).wait_recv()

    def ag_arrived(block, piece):
        ag_copy(block, 0, piece, lax.rem(me + 1, n_ep)).wait_recv()

    def ways(act_fn, copy_of, up, down):
        if up:
            @pl.when(zi < outer - 1)
            def _():
                act_fn(copy_of(0, me + INNER))
        if down:
            @pl.when(zi > 0)
            def _():
                act_fn(copy_of(1, me - INNER))
        for j in range(1, INNER):
            act_fn(copy_of(1 + j, zi * INNER + lax.rem(yi + j, INNER)))

    def ag_own(piece, act_fn):
        ways(act_fn, lambda way, target: own_copy(way, piece, target), True, True)

    def ag_all(zb, piece, act_fn, up, down):
        block = zb * INNER + yi
        ways(act_fn, lambda way, target: ag_copy(block, way, piece, target), up, down)

    def source_of(j):
        return lax.rem(hi_rep + j // 2, halves) * 2 + lax.rem(core + j, 2)

    def ext_copy(k):
        target = lax.rem(hi_rep + 1, halves) * 2 + k
        return pltpu.make_async_remote_copy(
            src_ref=og_hbm.at[:, pl.ds(pl.multiple_of(target * part, LANES), ext)],
            dst_ref=xe.at[me, :, pl.ds(pl.multiple_of(core * ext, LANES), ext)],
            send_sem=ext_send.at[k], recv_sem=ext_recv.at[core],
            device_id={"rep": target}, device_id_type=MESH,
        )

    def ext_arrived(k):
        pltpu.make_async_remote_copy(
            src_ref=og_hbm.at[:, pl.ds(0, ext)],
            dst_ref=xe.at[me, :, pl.ds(k * ext, ext)],
            send_sem=ext_send.at[k], recv_sem=ext_recv.at[k],
            device_id={"rep": partner}, device_id_type=MESH,
        ).wait_recv()

    def xs_copy(block, j, own=False, skip=0):
        target = source_of(j)
        cols = pl.ds(pl.multiple_of(target * part + skip, LANES), part - skip)
        return pltpu.make_async_remote_copy(
            src_ref=og_hbm.at[:, cols] if own else xg.at[block, :, cols],
            dst_ref=xs.at[rep, block, :, pl.ds(skip, part - skip)],
            send_sem=xs_send.at[j, block], recv_sem=xs_recv.at[rep, block],
            device_id={"rep": target}, device_id_type=MESH,
        )

    def xs_each(act_fn, block, j, own=False):
        if ext and j > 1:
            to_helped = lax.rem(source_of(j), 2) == 1
            for here, skip in ((to_helped, ext), (~to_helped, 0)):
                @pl.when(here)
                def _():
                    act_fn(xs_copy(block, j, own, skip))
        else:
            act_fn(xs_copy(block, j, own))

    def xs_arrived(j, block, skip):
        source = source_of(j)
        ref = xs.at[source, block, :, pl.ds(skip, part - skip)]
        pltpu.make_async_remote_copy(
            src_ref=ref, dst_ref=ref,
            send_sem=xs_send.at[j, block], recv_sem=xs_recv.at[source, block],
            device_id={"rep": partner}, device_id_type=MESH,
        ).wait_recv()

    def xs_begin(block, piece):
        for j in reversed(range(1, n_rep)):
            @pl.when(source_of(j) // (n_rep // pieces) == piece)
            def _():
                xs_each(begin, block, j)

    def act_copy(target):
        return pltpu.make_async_remote_copy(
            src_ref=act_hbm, dst_ref=actg.at[rep],
            send_sem=act_send.at[target], recv_sem=act_recv.at[rep],
            device_id={"rep": target}, device_id_type=MESH,
        )

    def fw_copy(source):
        return pltpu.make_async_remote_copy(
            src_ref=actg.at[source], dst_ref=actg.at[source],
            send_sem=fw_send.at[source], recv_sem=act_recv.at[source],
            device_id={"rep": partner}, device_id_type=MESH,
        )

    def gs_copy(j):
        return pltpu.make_async_remote_copy(
            src_ref=gs.at[rep], dst_ref=gs.at[rep],
            send_sem=gs_send.at[j], recv_sem=gs_recv.at[rep],
            device_id={"rep": source_of(j)}, device_id_type=MESH,
        )

    if ext:
        ext_copy(1).start()
    ag_own(0, begin)
    for target in cross:
        act_copy(target).start()
    for piece in range(1, pieces):
        ag_own(piece, begin)
    for j in reversed(range(1, n_rep)):
        xs_each(begin, me, j, True)
    act_copy(partner).start()

    place_r = lax.broadcasted_iota(jnp.int32, (tok, LANES), 0)
    place_c = lax.broadcasted_iota(jnp.int32, (tok, LANES), 1)
    lane_of = jnp.where(place_c == place_r + lax.rem(me, per) * tok, 1.0, 0.0).astype(BF16)
    ids = ids_ref[...].astype(F32)
    gates = gate_ref[...]
    named_by = jnp.dot((ids + 1.0).astype(BF16), lane_of, preferred_element_type=F32)
    gate_by = jnp.dot(gates.astype(BF16), lane_of, preferred_element_type=F32)
    row = lax.broadcasted_iota(jnp.int32, (n_ep * sub, LANES), 0)
    line = jnp.where(lax.rem(row, sub) < loc, row // sub * loc + lax.rem(row, sub) + 1, -1)
    line = line.astype(F32)
    dense = jnp.zeros((n_ep * sub, LANES), F32)
    for k in range(topk):
        dense = jnp.where(line == named_by[k : k + 1, :], gate_by[k : k + 1, :], dense)
    dg[...] = dense.reshape(n_ep, sub, LANES)
    gg[me] = dg[me]
    for j in range(1, n_ep):
        rg_copy(j).start()

    def inside(z):
        return (z >= 0) & (z < outer)

    def lines(s):
        for piece in range(pieces):
            for way in (-1, 1):
                z = zi + way * s

                @pl.when(inside(z))
                def _():
                    ag_arrived(z * INNER + yi, piece)
                    ag_all(z, piece, begin, way < 0, way > 0)
                    xs_begin(z * INNER + yi, piece)

    def sides(z):
        for j in range(1, INNER):
            block = z * INNER + lax.rem(yi + j, INNER)
            for piece in range(pieces):
                ag_arrived(block, piece)
                xs_begin(block, piece)

    def back_copy(target):
        return pltpu.make_async_remote_copy(
            src_ref=yb.at[target], dst_ref=rb.at[me],
            send_sem=back_send.at[target], recv_sem=back_recv.at[me],
            device_id={"ep": target}, device_id_type=MESH,
        )

    def input_rows(s):
        side = lax.rem(yi + 1, INNER)
        first = s == 1
        slots = [
            (jnp.where(first, me, (zi - s + 1) * INNER + side), inside(zi - s + 1)),
            ((zi + s - 1) * INNER + side, inside(zi + s - 1)),
            ((zi - s) * INNER + yi, inside(zi - s)),
            ((zi + s) * INNER + yi, inside(zi + s)),
        ]
        some = functools.reduce(lambda a, b: a | b, [slot[1] for slot in slots])

        @pl.when(some)
        def _():
            any_block = slots[3][0]
            for block, valid in reversed(slots[:3]):
                any_block = jnp.where(valid, block, any_block)
            blocks = [jnp.where(valid, block, any_block) for block, valid in slots]
            x = jnp.concatenate([xg[block] for block in blocks], axis=0)
            for e in range(loc):
                y = jnp.dot(x, wv[e], preferred_element_type=F32).astype(BF16)
                for k, block in enumerate(blocks):
                    yb[block, e] = y[k * tok : (k + 1) * tok]
            for block, valid in slots:
                @pl.when(valid & (block != me))
                def _():
                    back_copy(block).start()

    group = min(GROUP, n_ep)
    tiles = group // per
    slots = per * cap
    b_r = lax.broadcasted_iota(jnp.int32, (LANES, LANES), 0)
    b_c = lax.broadcasted_iota(jnp.int32, (LANES, LANES), 1)
    before = jnp.where((b_r // tok == b_c // tok) & (b_r < b_c), 1.0, 0.0).astype(BF16)
    p_r = lax.broadcasted_iota(jnp.int32, (slots, LANES), 0)
    p_c = lax.broadcasted_iota(jnp.int32, (slots, LANES), 1)
    offset = (p_r - p_c // tok * cap).astype(F32)

    def scale_rows(source, g, place):
        for q in range(tiles):
            gate = gs[source, g * tiles + q]
            named = jnp.where(gate > 0.0, 1.0, 0.0)
            slot = jnp.dot(named.astype(BF16), before, preferred_element_type=F32)
            for e in range(loc):
                pick = jnp.where(offset == slot[e : e + 1, :], gate[e : e + 1, :], 0.0)
                start = pl.multiple_of((g * tiles + q) * slots, 16)
                saved = actg[source, e, pl.ds(start, slots), :]
                at[place, e, pl.ds(q * LANES, LANES)] = transposed_dot(
                    pick.astype(BF16), saved
                ).astype(BF16)

    def act_arrived(source):
        fw_copy(source).wait_recv()

    def gs_arrived(j):
        source = source_of(j)
        pltpu.make_async_remote_copy(
            src_ref=gs.at[source], dst_ref=gs.at[source],
            send_sem=gs_send.at[j], recv_sem=gs_recv.at[source],
            device_id={"rep": source}, device_id_type=MESH,
        ).wait_recv()

    pairs = tok * topk
    t_r = lax.broadcasted_iota(jnp.int32, (pairs, tok), 0) // topk
    t_c = lax.broadcasted_iota(jnp.int32, (pairs, tok), 1)
    spread = jnp.where(t_r == t_c, 1.0, 0.0).astype(BF16)
    k_r = lax.rem(lax.broadcasted_iota(jnp.int32, (pairs, topk), 0), topk)
    k_c = lax.broadcasted_iota(jnp.int32, (pairs, topk), 1)

    def pair_column(values):
        rows = lax.dot_general(
            spread, values.astype(BF16), (((1,), (1,)), ((), ())), preferred_element_type=F32
        )
        return jnp.sum(jnp.where(k_r == k_c, rows, 0.0), axis=1, keepdims=True)

    span = group * loc * tok
    s_r = lax.broadcasted_iota(jnp.int32, (pairs, span), 0) // topk
    s_c = lax.broadcasted_iota(jnp.int32, (pairs, span), 1)
    same_token = s_r == lax.rem(s_c, tok)
    s_e = (s_c // tok).astype(F32)

    def choose():
        pair_id = pair_column(ids)
        high = gates.astype(BF16).astype(F32)
        pair_gate[...] = pair_column(high) + pair_column(gates - high)
        for g in range(n_ep // group):
            mine = same_token & (s_e + float(g * group * loc) == pair_id)
            chosen[g] = jnp.where(mine, 1.0, 0.0).astype(BF16)

    @pl.loop(1, outer + 1)
    def _(s):
        lines(s)

        @pl.when(s == 1)
        def _():
            for j in range(1, n_ep):
                source = lax.rem(me + j, n_ep)
                pltpu.make_async_remote_copy(
                    src_ref=gg.at[source], dst_ref=gg.at[source],
                    send_sem=rg_send.at[j], recv_sem=rg_recv.at[source],
                    device_id={"ep": source}, device_id_type=MESH,
                ).wait_recv()
            gs[rep] = jnp.sum(gg[...].reshape(n_ep // per, per, sub, LANES), axis=1)
            for j in range(1, n_rep):
                gs_copy(j).start()
            load_x.wait()
            load_w.wait()
            sides(zi)

        @pl.when(s > 1)
        def _():
            for way in (-1, 1):
                z = zi + way * (s - 1)

                @pl.when(inside(z))
                def _():
                    sides(z)

        input_rows(s)

        @pl.when(s == 2)
        def _():
            choose()
            if early:
                load_a.wait()
                scale_rows(rep, 0, 0)
                act_arrived(partner)
                gs_arrived(1)
                scale_rows(partner, 0, 1)

        if ext:
            @pl.when((s == EXT_STEP) & helped)
            def _():
                for k in range(2):
                    ext_arrived(k)
                for j in range(1, n_ep):
                    xe_copy(j).start()

    own_y = pltpu.make_async_copy(yb.at[me], rb.at[me], lsem.at[3])
    own_y.start()
    if not early:
        load_a.wait()

    for source in cross:
        act_arrived(source)
        fw_copy(source).start()

    if not early:
        act_arrived(partner)
        gs_arrived(1)
    for j in range(2, n_rep):
        gs_arrived(j)

    def x_own(g):
        cols = pl.ds(pl.multiple_of(rep * part, LANES), part)
        return xg[pl.ds(g * group, group), :, cols].reshape(group * tok, part)

    def x_near(source, g):
        return xs[source, pl.ds(g * group, group)].reshape(group * tok, part)

    def x_late(first, count, skip):
        return jnp.concatenate([
            xs[source_of(j), pl.ds(first, count), :, pl.ds(skip, part - skip)].reshape(
                count * tok, part - skip
            )
            for j in range(2, n_rep)
        ], axis=0)

    def at_late(e, first, count):
        rows = pl.ds(pl.multiple_of(first * tok, LANES // 2), count * tok)
        return jnp.concatenate([at[j, e, rows, :] for j in range(2, n_rep)], axis=0)

    def x_ext(source):
        cols = pl.ds(pl.multiple_of(lax.rem(source, 2) * ext, LANES), ext)
        return xe[:, :, cols].reshape(n_ep * tok, ext)

    def wait_blocks(j, skip, first=0, count=n_ep):
        @pl.loop(0, count)
        def _(k):
            xs_arrived(j, first + k, skip)

    def settle():
        for j in range(1, n_ep):
            rg_copy(j).wait_send()
        if ext:
            ext_copy(1).wait_send()

            @pl.when(helped)
            def _():
                for j in range(1, n_ep):
                    xe_copy(j).wait_send()
        for piece in range(pieces):
            ag_own(piece, end_send)
        for s in range(1, outer):
            @pl.when(zi - s >= 0)
            def _():
                for piece in range(pieces):
                    ag_all(zi - s, piece, end_send, True, False)

            @pl.when(zi + s < outer)
            def _():
                for piece in range(pieces):
                    ag_all(zi + s, piece, end_send, False, True)
        for target in cross + [partner]:
            act_copy(target).wait_send()
        for j in range(1, n_rep):
            gs_copy(j).wait_send()
        for source in cross:
            fw_copy(source).wait_send()

    def settle_rows(first, count):
        @pl.loop(0, count)
        def _(k):
            for j in range(1, n_rep):
                xs_each(end_send, first + k, j)

    def settle_back():
        for j in range(1, n_ep):
            back_copy(lax.rem(me + j, n_ep)).wait_send()

    def far_products(skip):
        if skip:
            for j in range(1, n_ep):
                xe_arrived(lax.rem(me + j, n_ep))
            for e in range(loc):
                term = acc[e, pl.ds(0, skip)]
                for j in range(2, n_rep):
                    term += transposed_dot(x_ext(source_of(j)), at[j, e])
                wg_ref[e, pl.ds(0, skip)] = term.astype(BF16)
        rest = pl.ds(skip, part - skip)
        late = INNER
        soon = jnp.where(zi >= outer // 2, late, 0)
        last = jnp.where(zi >= outer // 2, 0, n_ep - late)
        settle()
        for first, count in ((soon, n_ep - late), (last, late)):
            if count == late:
                settle_rows(soon, n_ep - late)
                settle_back()
            for j in range(2, n_rep):
                wait_blocks(j, skip, first, count)
            if count == late:
                settle_rows(last, late)
            x_part = x_late(first, count, skip)
            for e in range(loc):
                total = acc[e, rest] + transposed_dot(x_part, at_late(e, first, count))
                if count == late:
                    wg_ref[e, rest] = total.astype(BF16)
                else:
                    acc[e, rest] = total

    if early:
        for e in range(loc):
            acc[e] = transposed_dot(x_own(0), at[0, e])
        wait_blocks(1, 0)
        for e in range(loc):
            acc[e] += transposed_dot(x_near(partner, 0), at[1, e])
        for j in range(2, n_rep):
            if j % 2:
                act_arrived(source_of(j))
            scale_rows(source_of(j), 0, j)
        if ext:
            for here, skip in ((helped, ext), (~helped, 0)):
                @pl.when(here)
                def _():
                    far_products(skip)
        else:
            far_products(0)
    else:
        acc[...] = jnp.zeros_like(acc)

        @pl.loop(0, n_ep // group)
        def _(g):
            scale_rows(rep, g, 0)
            for e in range(loc):
                acc[e] += transposed_dot(x_own(g), at[0, e])

        @pl.loop(1, n_rep)
        def _(j):
            source = source_of(j)

            @pl.when((j > 1) & (lax.rem(j, 2) == 1))
            def _():
                act_arrived(source)

            @pl.loop(0, n_ep)
            def _(block):
                pltpu.make_async_remote_copy(
                    src_ref=xs.at[source, block], dst_ref=xs.at[source, block],
                    send_sem=xs_send.at[j, block], recv_sem=xs_recv.at[source, block],
                    device_id={"rep": partner}, device_id_type=MESH,
                ).wait_recv()

            @pl.loop(0, n_ep // group)
            def _(g):
                scale_rows(source, g, 0)
                for e in range(loc):
                    acc[e] += transposed_dot(x_near(source, g), at[0, e])

        wg_ref[...] = acc[...].astype(BF16)

    own_y.wait()
    for j in range(1, n_ep):
        source = lax.rem(me + j, n_ep)
        pltpu.make_async_remote_copy(
            src_ref=yb.at[source], dst_ref=rb.at[source],
            send_sem=back_send.at[j], recv_sem=back_recv.at[source],
            device_id={"ep": source}, device_id_type=MESH,
        ).wait_recv()
    total = jnp.zeros((pairs, hid), F32)
    for g in range(n_ep // group):
        total += jnp.dot(
            chosen[g],
            rb[g * group : (g + 1) * group].reshape(span, hid),
            preferred_element_type=F32,
        )
    ing_ref[...] = (total * pair_gate[...]).astype(ing_ref.dtype)

    if not early:
        settle()
        settle_rows(0, n_ep)
        settle_back()


def finish(in_v, w_v, in_out, w_out, sem):
    loc = w_v.shape[0]
    pairs = [(w_v.at[e], w_out.at[e]) for e in range(loc)] + [(in_v, in_out)]
    stores = [pltpu.make_async_copy(p[0], p[1], sem.at[k]) for k, p in enumerate(pairs)]
    for store in stores:
        store.start()
    for store in stores:
        store.wait()


def shards(out_grad, gate_weights, expert_ids, down_weight, act_cache):
    n_ep, n_rep = lax.axis_size("ep"), lax.axis_size("rep")
    tok, topk = expert_ids.shape
    loc, model, hid = down_weight.shape
    part = model // n_rep
    early = n_ep <= GROUP
    pieces = PIECES if early else 1
    ext = part // (4 * LANES) * LANES if n_rep == 4 and early else 0
    sub = pl.cdiv(loc, 8) * 8
    per = LANES // tok
    dma = pltpu.SemaphoreType.DMA
    vmem = pl.BlockSpec(memory_space=pltpu.VMEM)
    hbm = pl.BlockSpec(memory_space=pl.ANY)
    in_grad, weight_grad = pl.pallas_call(
        functools.partial(kernel, n_ep, n_rep, ext, pieces),
        out_shape=(
            pltpu.VMEM((tok * topk, hid), BF16),
            pltpu.VMEM((loc, part, hid), BF16),
        ),
        in_specs=[hbm, vmem, vmem, hbm, hbm],
        out_specs=(vmem, vmem),
        scratch_shapes=[
            pltpu.VMEM((n_ep, tok, model), BF16),
            pltpu.VMEM((n_ep, tok, max(2 * ext, LANES)), BF16),
            pltpu.VMEM((n_rep, n_ep, tok, part), BF16),
            pltpu.VMEM((n_ep, sub, LANES), F32),
            pltpu.VMEM((n_ep, sub, LANES), F32),
            pltpu.VMEM((n_rep, n_ep // per, sub, LANES), F32),
            pltpu.VMEM((n_rep,) + act_cache.shape, BF16),
            pltpu.VMEM((loc, model, hid), BF16),
            pltpu.VMEM((n_ep, loc, tok, hid), BF16),
            pltpu.VMEM((n_ep, loc, tok, hid), BF16),
            pltpu.VMEM((loc, part, hid), F32),
            pltpu.VMEM((n_rep if early else 1, loc, min(GROUP, n_ep) * tok, hid), BF16),
            pltpu.VMEM((n_ep // min(GROUP, n_ep), tok * topk, min(GROUP, n_ep) * loc * tok), BF16),
            pltpu.VMEM((tok * topk, 1), F32),
            dma((4,)), dma((1 + INNER, n_ep, pieces)), dma((n_ep, pieces)),
            dma((2,)), dma((2,)), dma((n_ep,)), dma((n_ep,)),
            dma((n_ep,)), dma((n_ep,)),
            dma((n_rep,)), dma((n_rep,)), dma((n_rep,)),
            dma((n_rep,)), dma((n_rep,)),
            dma((n_rep, n_ep)), dma((n_rep, n_ep)),
            dma((n_ep,)), dma((n_ep,)),
        ],
        compiler_params=pltpu.CompilerParams(
            collective_id=0, has_side_effects=True, vmem_limit_bytes=60 * 1024 * 1024
        ),
    )(out_grad, expert_ids.T, gate_weights.T, down_weight, act_cache)
    in_grad, weight_grad = pl.pallas_call(
        finish,
        out_shape=(
            jax.ShapeDtypeStruct((tok * topk, hid), BF16),
            jax.ShapeDtypeStruct((loc, part, hid), BF16),
        ),
        in_specs=[vmem, vmem],
        out_specs=(hbm, hbm),
        scratch_shapes=[dma((1 + loc,))],
        compiler_params=pltpu.CompilerParams(vmem_limit_bytes=1024 * 1024),
    )(
        pltpu.with_memory_space_constraint(in_grad, pltpu.VMEM),
        pltpu.with_memory_space_constraint(weight_grad, pltpu.VMEM),
    )
    return in_grad.reshape(tok, topk, hid), weight_grad


def solution(mesh):
    in_specs = (
        P(("ep", "rep"), None),
        P(("ep", "rep"), None),
        P(("ep", "rep"), None),
        P("ep", None, None),
        P("ep", "rep", None),
    )
    out_specs = (P(("ep", "rep"), None, None), P("ep", "rep", None))
    return jax.shard_map(shards, mesh=mesh, in_specs=in_specs, out_specs=out_specs, check_vma=False)
```

```python
import functools
import jax
import jax.numpy as jnp
from jax import lax
from jax.experimental import pallas as pl
from jax.experimental.pallas import tpu as pltpu
from jax.sharding import PartitionSpec as P

MESH = pl.DeviceIdType.MESH
F32 = jnp.float32
BF16 = jnp.bfloat16
INNER = 2
PIECES = 2
GROUP = 8
LANES = 128
EXT_STEP = 2


def transposed_dot(a, b):
    return lax.dot_general(a, b, (((0,), (0,)), ((), ())), preferred_element_type=F32)


def kernel(
    n_ep, n_rep, ext, pieces, og_hbm, ids_ref, gate_ref, w_hbm, act_hbm, ing_ref, wg_ref,
    xg, xe, xs, dg, gg, gs, actg, wv, yb, rb, acc, at, chosen, pair_gate,
    lsem, ag_send, ag_recv, ext_send, ext_recv, xe_send, xe_recv, rg_send, rg_recv,
    act_send, act_recv, fw_send, gs_send, gs_recv, xs_send, xs_recv, back_send, back_recv,
):
    topk, tok = ids_ref.shape
    model = og_hbm.shape[1]
    loc, _, hid = w_hbm.shape
    part = xs.shape[3]
    cap = act_hbm.shape[1] // n_ep
    outer = n_ep // INNER
    half = model // pieces
    sub = dg.shape[1]
    per = LANES // tok
    me = lax.axis_index("ep")
    rep = lax.axis_index("rep")
    zi, yi = me // INNER, lax.rem(me, INNER)
    hi_rep, core = rep // 2, lax.rem(rep, 2)
    halves = n_rep // 2
    cross = [lax.rem(hi_rep + j, halves) * 2 + core for j in range(1, halves)]
    partner = hi_rep * 2 + 1 - core
    early = n_ep <= GROUP
    helped = core == 1

    barrier = pltpu.get_barrier_semaphore()
    for j in range(1, n_ep):
        pl.semaphore_signal(
            barrier, inc=1, device_id={"ep": lax.rem(me + j, n_ep)}, device_id_type=MESH
        )
    for j in range(1, n_rep):
        pl.semaphore_signal(
            barrier, inc=1, device_id={"rep": lax.rem(rep + j, n_rep)}, device_id_type=MESH
        )

    load_x = pltpu.make_async_copy(og_hbm, xg.at[me], lsem.at[0])
    load_a = pltpu.make_async_copy(act_hbm, actg.at[rep], lsem.at[1])
    load_w = pltpu.make_async_copy(w_hbm, wv, lsem.at[2])

    pl.semaphore_wait(barrier, n_ep - 1 + n_rep - 1)

    def begin(copy):
        copy.start()

    def end_send(copy):
        copy.wait_send()

    def rg_copy(j):
        target = lax.rem(me + j, n_ep)
        return pltpu.make_async_remote_copy(
            src_ref=dg.at[target], dst_ref=gg.at[me],
            send_sem=rg_send.at[j], recv_sem=rg_recv.at[me],
            device_id={"ep": target}, device_id_type=MESH,
        )

    def ag_copy(block, way, piece, target):
        cols = pl.ds(piece * half, half)
        return pltpu.make_async_remote_copy(
            src_ref=xg.at[block, :, cols], dst_ref=xg.at[block, :, cols],
            send_sem=ag_send.at[way, block, piece], recv_sem=ag_recv.at[block, piece],
            device_id={"ep": target}, device_id_type=MESH,
        )

    def own_copy(way, piece, target):
        cols = pl.ds(piece * half, half)
        return pltpu.make_async_remote_copy(
            src_ref=og_hbm.at[:, cols], dst_ref=xg.at[me, :, cols],
            send_sem=ag_send.at[way, me, piece], recv_sem=ag_recv.at[me, piece],
            device_id={"ep": target}, device_id_type=MESH,
        )

    def xe_copy(j):
        return pltpu.make_async_remote_copy(
            src_ref=xe.at[me], dst_ref=xe.at[me],
            send_sem=xe_send.at[j], recv_sem=xe_recv.at[me],
            device_id={"ep": lax.rem(me + j, n_ep)}, device_id_type=MESH,
        )

    def xe_arrived(block):
        pltpu.make_async_remote_copy(
            src_ref=xe.at[block], dst_ref=xe.at[block],
            send_sem=xe_send.at[0], recv_sem=xe_recv.at[block],
            device_id={"ep": lax.rem(me + 1, n_ep)}, device_id_type=MESH,
        ).wait_recv()

    def ag_arrived(block, piece):
        ag_copy(block, 0, piece, lax.rem(me + 1, n_ep)).wait_recv()

    def ways(act_fn, copy_of, up, down):
        if up:
            @pl.when(zi < outer - 1)
            def _():
                act_fn(copy_of(0, me + INNER))
        if down:
            @pl.when(zi > 0)
            def _():
                act_fn(copy_of(1, me - INNER))
        for j in range(1, INNER):
            act_fn(copy_of(1 + j, zi * INNER + lax.rem(yi + j, INNER)))

    def ag_own(piece, act_fn):
        ways(act_fn, lambda way, target: own_copy(way, piece, target), True, True)

    def ag_all(zb, piece, act_fn, up, down):
        block = zb * INNER + yi
        ways(act_fn, lambda way, target: ag_copy(block, way, piece, target), up, down)

    def source_of(j):
        return lax.rem(hi_rep + j // 2, halves) * 2 + lax.rem(core + j, 2)

    def ext_copy(k):
        target = lax.rem(hi_rep + 1, halves) * 2 + k
        return pltpu.make_async_remote_copy(
            src_ref=og_hbm.at[:, pl.ds(pl.multiple_of(target * part, LANES), ext)],
            dst_ref=xe.at[me, :, pl.ds(pl.multiple_of(core * ext, LANES), ext)],
            send_sem=ext_send.at[k], recv_sem=ext_recv.at[core],
            device_id={"rep": target}, device_id_type=MESH,
        )

    def ext_arrived(k):
        pltpu.make_async_remote_copy(
            src_ref=og_hbm.at[:, pl.ds(0, ext)],
            dst_ref=xe.at[me, :, pl.ds(k * ext, ext)],
            send_sem=ext_send.at[k], recv_sem=ext_recv.at[k],
            device_id={"rep": partner}, device_id_type=MESH,
        ).wait_recv()

    def xs_copy(block, j, own=False, skip=0):
        target = source_of(j)
        cols = pl.ds(pl.multiple_of(target * part + skip, LANES), part - skip)
        return pltpu.make_async_remote_copy(
            src_ref=og_hbm.at[:, cols] if own else xg.at[block, :, cols],
            dst_ref=xs.at[rep, block, :, pl.ds(skip, part - skip)],
            send_sem=xs_send.at[j, block], recv_sem=xs_recv.at[rep, block],
            device_id={"rep": target}, device_id_type=MESH,
        )

    def xs_each(act_fn, block, j, own=False):
        if ext and j > 1:
            to_helped = lax.rem(source_of(j), 2) == 1
            for here, skip in ((to_helped, ext), (~to_helped, 0)):
                @pl.when(here)
                def _():
                    act_fn(xs_copy(block, j, own, skip))
        else:
            act_fn(xs_copy(block, j, own))

    def xs_arrived(j, block, skip):
        source = source_of(j)
        ref = xs.at[source, block, :, pl.ds(skip, part - skip)]
        pltpu.make_async_remote_copy(
            src_ref=ref, dst_ref=ref,
            send_sem=xs_send.at[j, block], recv_sem=xs_recv.at[source, block],
            device_id={"rep": partner}, device_id_type=MESH,
        ).wait_recv()

    def xs_begin(block, piece):
        for j in reversed(range(1, n_rep)):
            @pl.when(source_of(j) // (n_rep // pieces) == piece)
            def _():
                xs_each(begin, block, j)

    def act_copy(target):
        return pltpu.make_async_remote_copy(
            src_ref=act_hbm, dst_ref=actg.at[rep],
            send_sem=act_send.at[target], recv_sem=act_recv.at[rep],
            device_id={"rep": target}, device_id_type=MESH,
        )

    def fw_copy(source):
        return pltpu.make_async_remote_copy(
            src_ref=actg.at[source], dst_ref=actg.at[source],
            send_sem=fw_send.at[source], recv_sem=act_recv.at[source],
            device_id={"rep": partner}, device_id_type=MESH,
        )

    def gs_copy(j):
        return pltpu.make_async_remote_copy(
            src_ref=gs.at[rep], dst_ref=gs.at[rep],
            send_sem=gs_send.at[j], recv_sem=gs_recv.at[rep],
            device_id={"rep": source_of(j)}, device_id_type=MESH,
        )

    if ext:
        ext_copy(1).start()
    ag_own(0, begin)
    for target in cross:
        act_copy(target).start()
    for piece in range(1, pieces):
        ag_own(piece, begin)
    for j in reversed(range(1, n_rep)):
        xs_each(begin, me, j, True)
    act_copy(partner).start()
    load_x.start()
    load_w.start()
    load_a.start()

    place_r = lax.broadcasted_iota(jnp.int32, (tok, LANES), 0)
    place_c = lax.broadcasted_iota(jnp.int32, (tok, LANES), 1)
    lane_of = jnp.where(place_c == place_r + lax.rem(me, per) * tok, 1.0, 0.0).astype(BF16)
    ids = ids_ref[...].astype(F32)
    gates = gate_ref[...]
    named_by = jnp.dot((ids + 1.0).astype(BF16), lane_of, preferred_element_type=F32)
    gate_by = jnp.dot(gates.astype(BF16), lane_of, preferred_element_type=F32)
    row = lax.broadcasted_iota(jnp.int32, (n_ep * sub, LANES), 0)
    line = jnp.where(lax.rem(row, sub) < loc, row // sub * loc + lax.rem(row, sub) + 1, -1)
    line = line.astype(F32)
    dense = jnp.zeros((n_ep * sub, LANES), F32)
    for k in range(topk):
        dense = jnp.where(line == named_by[k : k + 1, :], gate_by[k : k + 1, :], dense)
    dg[...] = dense.reshape(n_ep, sub, LANES)
    gg[me] = dg[me]
    for j in range(1, n_ep):
        rg_copy(j).start()

    def inside(z):
        return (z >= 0) & (z < outer)

    def lines(s):
        for piece in range(pieces):
            for way in (-1, 1):
                z = zi + way * s

                @pl.when(inside(z))
                def _():
                    ag_arrived(z * INNER + yi, piece)
                    ag_all(z, piece, begin, way < 0, way > 0)
                    xs_begin(z * INNER + yi, piece)

    def sides(z):
        for j in range(1, INNER):
            block = z * INNER + lax.rem(yi + j, INNER)
            for piece in range(pieces):
                ag_arrived(block, piece)
                xs_begin(block, piece)

    def back_copy(target):
        return pltpu.make_async_remote_copy(
            src_ref=yb.at[target], dst_ref=rb.at[me],
            send_sem=back_send.at[target], recv_sem=back_recv.at[me],
            device_id={"ep": target}, device_id_type=MESH,
        )

    def input_rows(s):
        side = lax.rem(yi + 1, INNER)
        first = s == 1
        slots = [
            (jnp.where(first, me, (zi - s + 1) * INNER + side), inside(zi - s + 1)),
            ((zi + s - 1) * INNER + side, inside(zi + s - 1)),
            ((zi - s) * INNER + yi, inside(zi - s)),
            ((zi + s) * INNER + yi, inside(zi + s)),
        ]
        some = functools.reduce(lambda a, b: a | b, [slot[1] for slot in slots])

        @pl.when(some)
        def _():
            any_block = slots[3][0]
            for block, valid in reversed(slots[:3]):
                any_block = jnp.where(valid, block, any_block)
            blocks = [jnp.where(valid, block, any_block) for block, valid in slots]
            x = jnp.concatenate([xg[block] for block in blocks], axis=0)
            for e in range(loc):
                y = jnp.dot(x, wv[e], preferred_element_type=F32).astype(BF16)
                for k, block in enumerate(blocks):
                    yb[block, e] = y[k * tok : (k + 1) * tok]
            for block, valid in slots:
                @pl.when(valid & (block != me))
                def _():
                    back_copy(block).start()

    group = min(GROUP, n_ep)
    tiles = group // per
    slots = per * cap
    b_r = lax.broadcasted_iota(jnp.int32, (LANES, LANES), 0)
    b_c = lax.broadcasted_iota(jnp.int32, (LANES, LANES), 1)
    before = jnp.where((b_r // tok == b_c // tok) & (b_r < b_c), 1.0, 0.0).astype(BF16)
    p_r = lax.broadcasted_iota(jnp.int32, (slots, LANES), 0)
    p_c = lax.broadcasted_iota(jnp.int32, (slots, LANES), 1)
    offset = (p_r - p_c // tok * cap).astype(F32)

    def scale_rows(source, g, place):
        for q in range(tiles):
            gate = gs[source, g * tiles + q]
            named = jnp.where(gate > 0.0, 1.0, 0.0)
            slot = jnp.dot(named.astype(BF16), before, preferred_element_type=F32)
            for e in range(loc):
                pick = jnp.where(offset == slot[e : e + 1, :], gate[e : e + 1, :], 0.0)
                start = pl.multiple_of((g * tiles + q) * slots, 16)
                saved = actg[source, e, pl.ds(start, slots), :]
                at[place, e, pl.ds(q * LANES, LANES)] = transposed_dot(
                    pick.astype(BF16), saved
                ).astype(BF16)

    def act_arrived(source):
        fw_copy(source).wait_recv()

    def gs_arrived(j):
        source = source_of(j)
        pltpu.make_async_remote_copy(
            src_ref=gs.at[source], dst_ref=gs.at[source],
            send_sem=gs_send.at[j], recv_sem=gs_recv.at[source],
            device_id={"rep": source}, device_id_type=MESH,
        ).wait_recv()

    pairs = tok * topk
    t_r = lax.broadcasted_iota(jnp.int32, (pairs, tok), 0) // topk
    t_c = lax.broadcasted_iota(jnp.int32, (pairs, tok), 1)
    spread = jnp.where(t_r == t_c, 1.0, 0.0).astype(BF16)
    k_r = lax.rem(lax.broadcasted_iota(jnp.int32, (pairs, topk), 0), topk)
    k_c = lax.broadcasted_iota(jnp.int32, (pairs, topk), 1)

    def pair_column(values):
        rows = lax.dot_general(
            spread, values.astype(BF16), (((1,), (1,)), ((), ())), preferred_element_type=F32
        )
        return jnp.sum(jnp.where(k_r == k_c, rows, 0.0), axis=1, keepdims=True)

    span = group * loc * tok
    s_r = lax.broadcasted_iota(jnp.int32, (pairs, span), 0) // topk
    s_c = lax.broadcasted_iota(jnp.int32, (pairs, span), 1)
    same_token = s_r == lax.rem(s_c, tok)
    s_e = (s_c // tok).astype(F32)

    def choose():
        pair_id = pair_column(ids)
        high = gates.astype(BF16).astype(F32)
        pair_gate[...] = pair_column(high) + pair_column(gates - high)
        for g in range(n_ep // group):
            mine = same_token & (s_e + float(g * group * loc) == pair_id)
            chosen[g] = jnp.where(mine, 1.0, 0.0).astype(BF16)

    @pl.loop(1, outer + 1)
    def _(s):
        lines(s)

        @pl.when(s == 1)
        def _():
            for j in range(1, n_ep):
                source = lax.rem(me + j, n_ep)
                pltpu.make_async_remote_copy(
                    src_ref=gg.at[source], dst_ref=gg.at[source],
                    send_sem=rg_send.at[j], recv_sem=rg_recv.at[source],
                    device_id={"ep": source}, device_id_type=MESH,
                ).wait_recv()
            gs[rep] = jnp.sum(gg[...].reshape(n_ep // per, per, sub, LANES), axis=1)
            for j in range(1, n_rep):
                gs_copy(j).start()
            load_x.wait()
            load_w.wait()
            sides(zi)

        @pl.when(s > 1)
        def _():
            for way in (-1, 1):
                z = zi + way * (s - 1)

                @pl.when(inside(z))
                def _():
                    sides(z)

        input_rows(s)

        @pl.when(s == 2)
        def _():
            choose()
            if early:
                load_a.wait()
                scale_rows(rep, 0, 0)
                act_arrived(partner)
                gs_arrived(1)
                scale_rows(partner, 0, 1)

        if ext:
            @pl.when((s == EXT_STEP) & helped)
            def _():
                for k in range(2):
                    ext_arrived(k)
                for j in range(1, n_ep):
                    xe_copy(j).start()

    own_y = pltpu.make_async_copy(yb.at[me], rb.at[me], lsem.at[3])
    own_y.start()
    if not early:
        load_a.wait()

    for source in cross:
        act_arrived(source)
        fw_copy(source).start()

    if not early:
        act_arrived(partner)
        gs_arrived(1)
    for j in range(2, n_rep):
        gs_arrived(j)

    def x_own(g):
        cols = pl.ds(pl.multiple_of(rep * part, LANES), part)
        return xg[pl.ds(g * group, group), :, cols].reshape(group * tok, part)

    def x_near(source, g):
        return xs[source, pl.ds(g * group, group)].reshape(group * tok, part)

    def x_late(first, count, skip):
        return jnp.concatenate([
            xs[source_of(j), pl.ds(first, count), :, pl.ds(skip, part - skip)].reshape(
                count * tok, part - skip
            )
            for j in range(2, n_rep)
        ], axis=0)

    def at_late(e, first, count):
        rows = pl.ds(pl.multiple_of(first * tok, LANES // 2), count * tok)
        return jnp.concatenate([at[j, e, rows, :] for j in range(2, n_rep)], axis=0)

    def x_ext(source):
        cols = pl.ds(pl.multiple_of(lax.rem(source, 2) * ext, LANES), ext)
        return xe[:, :, cols].reshape(n_ep * tok, ext)

    def wait_blocks(j, skip, first=0, count=n_ep):
        @pl.loop(0, count)
        def _(k):
            xs_arrived(j, first + k, skip)

    def settle():
        for j in range(1, n_ep):
            rg_copy(j).wait_send()
        if ext:
            ext_copy(1).wait_send()

            @pl.when(helped)
            def _():
                for j in range(1, n_ep):
                    xe_copy(j).wait_send()
        for piece in range(pieces):
            ag_own(piece, end_send)
        for s in range(1, outer):
            @pl.when(zi - s >= 0)
            def _():
                for piece in range(pieces):
                    ag_all(zi - s, piece, end_send, True, False)

            @pl.when(zi + s < outer)
            def _():
                for piece in range(pieces):
                    ag_all(zi + s, piece, end_send, False, True)
        for target in cross + [partner]:
            act_copy(target).wait_send()
        for j in range(1, n_rep):
            gs_copy(j).wait_send()
        for source in cross:
            fw_copy(source).wait_send()

    def settle_rows(first, count):
        @pl.loop(0, count)
        def _(k):
            for j in range(1, n_rep):
                xs_each(end_send, first + k, j)

    def settle_back():
        for j in range(1, n_ep):
            back_copy(lax.rem(me + j, n_ep)).wait_send()

    def far_products(skip):
        if skip:
            for j in range(1, n_ep):
                xe_arrived(lax.rem(me + j, n_ep))
            for e in range(loc):
                term = acc[e, pl.ds(0, skip)]
                for j in range(2, n_rep):
                    term += transposed_dot(x_ext(source_of(j)), at[j, e])
                wg_ref[e, pl.ds(0, skip)] = term.astype(BF16)
        rest = pl.ds(skip, part - skip)
        late = INNER
        soon = jnp.where(zi >= outer // 2, late, 0)
        last = jnp.where(zi >= outer // 2, 0, n_ep - late)
        settle()
        for first, count in ((soon, n_ep - late), (last, late)):
            if count == late:
                settle_rows(soon, n_ep - late)
            for j in range(2, n_rep):
                wait_blocks(j, skip, first, count)
            if count == late:
                settle_rows(last, late)
                settle_back()
            x_part = x_late(first, count, skip)
            for e in range(loc):
                total = acc[e, rest] + transposed_dot(x_part, at_late(e, first, count))
                if count == late:
                    wg_ref[e, rest] = total.astype(BF16)
                else:
                    acc[e, rest] = total

    if early:
        for e in range(loc):
            acc[e] = transposed_dot(x_own(0), at[0, e])
        wait_blocks(1, 0)
        for e in range(loc):
            acc[e] += transposed_dot(x_near(partner, 0), at[1, e])
        for j in range(2, n_rep):
            if j % 2:
                act_arrived(source_of(j))
            scale_rows(source_of(j), 0, j)
        if ext:
            for here, skip in ((helped, ext), (~helped, 0)):
                @pl.when(here)
                def _():
                    far_products(skip)
        else:
            far_products(0)
    else:
        acc[...] = jnp.zeros_like(acc)

        @pl.loop(0, n_ep // group)
        def _(g):
            scale_rows(rep, g, 0)
            for e in range(loc):
                acc[e] += transposed_dot(x_own(g), at[0, e])

        @pl.loop(1, n_rep)
        def _(j):
            source = source_of(j)

            @pl.when((j > 1) & (lax.rem(j, 2) == 1))
            def _():
                act_arrived(source)

            @pl.loop(0, n_ep)
            def _(block):
                pltpu.make_async_remote_copy(
                    src_ref=xs.at[source, block], dst_ref=xs.at[source, block],
                    send_sem=xs_send.at[j, block], recv_sem=xs_recv.at[source, block],
                    device_id={"rep": partner}, device_id_type=MESH,
                ).wait_recv()

            @pl.loop(0, n_ep // group)
            def _(g):
                scale_rows(source, g, 0)
                for e in range(loc):
                    acc[e] += transposed_dot(x_near(source, g), at[0, e])

        wg_ref[...] = acc[...].astype(BF16)

    own_y.wait()
    for j in range(1, n_ep):
        source = lax.rem(me + j, n_ep)
        pltpu.make_async_remote_copy(
            src_ref=yb.at[source], dst_ref=rb.at[source],
            send_sem=back_send.at[j], recv_sem=back_recv.at[source],
            device_id={"ep": source}, device_id_type=MESH,
        ).wait_recv()
    total = jnp.zeros((pairs, hid), F32)
    for g in range(n_ep // group):
        total += jnp.dot(
            chosen[g],
            rb[g * group : (g + 1) * group].reshape(span, hid),
            preferred_element_type=F32,
        )
    ing_ref[...] = (total * pair_gate[...]).astype(ing_ref.dtype)

    if not early:
        settle()
        settle_rows(0, n_ep)
        settle_back()


def finish(in_v, w_v, in_out, w_out, sem):
    loc = w_v.shape[0]
    pairs = [(w_v.at[e], w_out.at[e]) for e in range(loc)] + [(in_v, in_out)]
    stores = [pltpu.make_async_copy(p[0], p[1], sem.at[k]) for k, p in enumerate(pairs)]
    for store in stores:
        store.start()
    for store in stores:
        store.wait()


def shards(out_grad, gate_weights, expert_ids, down_weight, act_cache):
    n_ep, n_rep = lax.axis_size("ep"), lax.axis_size("rep")
    tok, topk = expert_ids.shape
    loc, model, hid = down_weight.shape
    part = model // n_rep
    early = n_ep <= GROUP
    pieces = PIECES if early else 1
    ext = part // (4 * LANES) * LANES if n_rep == 4 and early else 0
    sub = pl.cdiv(loc, 8) * 8
    per = LANES // tok
    dma = pltpu.SemaphoreType.DMA
    vmem = pl.BlockSpec(memory_space=pltpu.VMEM)
    hbm = pl.BlockSpec(memory_space=pl.ANY)
    in_grad, weight_grad = pl.pallas_call(
        functools.partial(kernel, n_ep, n_rep, ext, pieces),
        out_shape=(
            pltpu.VMEM((tok * topk, hid), BF16),
            pltpu.VMEM((loc, part, hid), BF16),
        ),
        in_specs=[hbm, vmem, vmem, hbm, hbm],
        out_specs=(vmem, vmem),
        scratch_shapes=[
            pltpu.VMEM((n_ep, tok, model), BF16),
            pltpu.VMEM((n_ep, tok, max(2 * ext, LANES)), BF16),
            pltpu.VMEM((n_rep, n_ep, tok, part), BF16),
            pltpu.VMEM((n_ep, sub, LANES), F32),
            pltpu.VMEM((n_ep, sub, LANES), F32),
            pltpu.VMEM((n_rep, n_ep // per, sub, LANES), F32),
            pltpu.VMEM((n_rep,) + act_cache.shape, BF16),
            pltpu.VMEM((loc, model, hid), BF16),
            pltpu.VMEM((n_ep, loc, tok, hid), BF16),
            pltpu.VMEM((n_ep, loc, tok, hid), BF16),
            pltpu.VMEM((loc, part, hid), F32),
            pltpu.VMEM((n_rep if early else 1, loc, min(GROUP, n_ep) * tok, hid), BF16),
            pltpu.VMEM((n_ep // min(GROUP, n_ep), tok * topk, min(GROUP, n_ep) * loc * tok), BF16),
            pltpu.VMEM((tok * topk, 1), F32),
            dma((4,)), dma((1 + INNER, n_ep, pieces)), dma((n_ep, pieces)),
            dma((2,)), dma((2,)), dma((n_ep,)), dma((n_ep,)),
            dma((n_ep,)), dma((n_ep,)),
            dma((n_rep,)), dma((n_rep,)), dma((n_rep,)),
            dma((n_rep,)), dma((n_rep,)),
            dma((n_rep, n_ep)), dma((n_rep, n_ep)),
            dma((n_ep,)), dma((n_ep,)),
        ],
        compiler_params=pltpu.CompilerParams(
            collective_id=0, has_side_effects=True, vmem_limit_bytes=60 * 1024 * 1024
        ),
    )(out_grad, expert_ids.T, gate_weights.T, down_weight, act_cache)
    in_grad, weight_grad = pl.pallas_call(
        finish,
        out_shape=(
            jax.ShapeDtypeStruct((tok * topk, hid), BF16),
            jax.ShapeDtypeStruct((loc, part, hid), BF16),
        ),
        in_specs=[vmem, vmem],
        out_specs=(hbm, hbm),
        scratch_shapes=[dma((1 + loc,))],
        compiler_params=pltpu.CompilerParams(vmem_limit_bytes=1024 * 1024),
    )(
        pltpu.with_memory_space_constraint(in_grad, pltpu.VMEM),
        pltpu.with_memory_space_constraint(weight_grad, pltpu.VMEM),
    )
    return in_grad.reshape(tok, topk, hid), weight_grad


def solution(mesh):
    in_specs = (
        P(("ep", "rep"), None),
        P(("ep", "rep"), None),
        P(("ep", "rep"), None),
        P("ep", None, None),
        P("ep", "rep", None),
    )
    out_specs = (P(("ep", "rep"), None, None), P("ep", "rep", None))
    return jax.shard_map(shards, mesh=mesh, in_specs=in_specs, out_specs=out_specs, check_vma=False)
```

```python
import functools
import jax
import jax.numpy as jnp
from jax import lax
from jax.experimental import pallas as pl
from jax.experimental.pallas import tpu as pltpu
from jax.sharding import PartitionSpec as P

MESH = pl.DeviceIdType.MESH
F32 = jnp.float32
BF16 = jnp.bfloat16
INNER = 2
PIECES = 2
GROUP = 8
LANES = 128
EXT_STEP = 2


def transposed_dot(a, b):
    return lax.dot_general(a, b, (((0,), (0,)), ((), ())), preferred_element_type=F32)


def kernel(
    n_ep, n_rep, ext, pieces, og_hbm, ids_ref, gate_ref, w_hbm, act_hbm, ing_ref, wg_ref,
    xg, xe, xs, dg, gg, gs, actg, wv, yb, rb, acc, at, chosen, pair_gate,
    lsem, ag_send, ag_recv, ext_send, ext_recv, xe_send, xe_recv, rg_send, rg_recv,
    act_send, act_recv, fw_send, gs_send, gs_recv, xs_send, xs_recv, back_send, back_recv,
):
    topk, tok = ids_ref.shape
    model = og_hbm.shape[1]
    loc, _, hid = w_hbm.shape
    part = xs.shape[3]
    cap = act_hbm.shape[1] // n_ep
    outer = n_ep // INNER
    half = model // pieces
    sub = dg.shape[1]
    per = LANES // tok
    me = lax.axis_index("ep")
    rep = lax.axis_index("rep")
    zi, yi = me // INNER, lax.rem(me, INNER)
    hi_rep, core = rep // 2, lax.rem(rep, 2)
    halves = n_rep // 2
    cross = [lax.rem(hi_rep + j, halves) * 2 + core for j in range(1, halves)]
    partner = hi_rep * 2 + 1 - core
    early = n_ep <= GROUP
    helped = core == 1

    barrier = pltpu.get_barrier_semaphore()
    for j in range(1, n_ep):
        pl.semaphore_signal(
            barrier, inc=1, device_id={"ep": lax.rem(me + j, n_ep)}, device_id_type=MESH
        )
    for j in range(1, n_rep):
        pl.semaphore_signal(
            barrier, inc=1, device_id={"rep": lax.rem(rep + j, n_rep)}, device_id_type=MESH
        )

    load_x = pltpu.make_async_copy(og_hbm, xg.at[me], lsem.at[0])
    load_x.start()
    load_a = pltpu.make_async_copy(act_hbm, actg.at[rep], lsem.at[1])
    load_a.start()
    load_w = pltpu.make_async_copy(w_hbm, wv, lsem.at[2])
    load_w.start()

    pl.semaphore_wait(barrier, n_ep - 1 + n_rep - 1)

    def begin(copy):
        copy.start()

    def end_send(copy):
        copy.wait_send()

    def rg_copy(j):
        target = lax.rem(me + j, n_ep)
        return pltpu.make_async_remote_copy(
            src_ref=dg.at[target], dst_ref=gg.at[me],
            send_sem=rg_send.at[j], recv_sem=rg_recv.at[me],
            device_id={"ep": target}, device_id_type=MESH,
        )

    def ag_copy(block, way, piece, target):
        cols = pl.ds(piece * half, half)
        return pltpu.make_async_remote_copy(
            src_ref=xg.at[block, :, cols], dst_ref=xg.at[block, :, cols],
            send_sem=ag_send.at[way, block, piece], recv_sem=ag_recv.at[block, piece],
            device_id={"ep": target}, device_id_type=MESH,
        )

    def own_copy(way, piece, target):
        cols = pl.ds(piece * half, half)
        return pltpu.make_async_remote_copy(
            src_ref=og_hbm.at[:, cols], dst_ref=xg.at[me, :, cols],
            send_sem=ag_send.at[way, me, piece], recv_sem=ag_recv.at[me, piece],
            device_id={"ep": target}, device_id_type=MESH,
        )

    def xe_copy(j):
        return pltpu.make_async_remote_copy(
            src_ref=xe.at[me], dst_ref=xe.at[me],
            send_sem=xe_send.at[j], recv_sem=xe_recv.at[me],
            device_id={"ep": lax.rem(me + j, n_ep)}, device_id_type=MESH,
        )

    def xe_arrived(block):
        pltpu.make_async_remote_copy(
            src_ref=xe.at[block], dst_ref=xe.at[block],
            send_sem=xe_send.at[0], recv_sem=xe_recv.at[block],
            device_id={"ep": lax.rem(me + 1, n_ep)}, device_id_type=MESH,
        ).wait_recv()

    def ag_arrived(block, piece):
        ag_copy(block, 0, piece, lax.rem(me + 1, n_ep)).wait_recv()

    def ways(act_fn, copy_of, up, down):
        if up:
            @pl.when(zi < outer - 1)
            def _():
                act_fn(copy_of(0, me + INNER))
        if down:
            @pl.when(zi > 0)
            def _():
                act_fn(copy_of(1, me - INNER))
        for j in range(1, INNER):
            act_fn(copy_of(1 + j, zi * INNER + lax.rem(yi + j, INNER)))

    def ag_own(piece, act_fn):
        ways(act_fn, lambda way, target: own_copy(way, piece, target), True, True)

    def ag_all(zb, piece, act_fn, up, down):
        block = zb * INNER + yi
        ways(act_fn, lambda way, target: ag_copy(block, way, piece, target), up, down)

    def source_of(j):
        return lax.rem(hi_rep + j // 2, halves) * 2 + lax.rem(core + j, 2)

    def ext_copy(k):
        target = lax.rem(hi_rep + 1, halves) * 2 + k
        return pltpu.make_async_remote_copy(
            src_ref=og_hbm.at[:, pl.ds(pl.multiple_of(target * part, LANES), ext)],
            dst_ref=xe.at[me, :, pl.ds(pl.multiple_of(core * ext, LANES), ext)],
            send_sem=ext_send.at[k], recv_sem=ext_recv.at[core],
            device_id={"rep": target}, device_id_type=MESH,
        )

    def ext_arrived(k):
        pltpu.make_async_remote_copy(
            src_ref=og_hbm.at[:, pl.ds(0, ext)],
            dst_ref=xe.at[me, :, pl.ds(k * ext, ext)],
            send_sem=ext_send.at[k], recv_sem=ext_recv.at[k],
            device_id={"rep": partner}, device_id_type=MESH,
        ).wait_recv()

    def xs_copy(block, j, own=False, skip=0):
        target = source_of(j)
        cols = pl.ds(pl.multiple_of(target * part + skip, LANES), part - skip)
        return pltpu.make_async_remote_copy(
            src_ref=og_hbm.at[:, cols] if own else xg.at[block, :, cols],
            dst_ref=xs.at[rep, block, :, pl.ds(skip, part - skip)],
            send_sem=xs_send.at[j, block], recv_sem=xs_recv.at[rep, block],
            device_id={"rep": target}, device_id_type=MESH,
        )

    def xs_each(act_fn, block, j, own=False):
        if ext and j > 1:
            to_helped = lax.rem(source_of(j), 2) == 1
            for here, skip in ((to_helped, ext), (~to_helped, 0)):
                @pl.when(here)
                def _():
                    act_fn(xs_copy(block, j, own, skip))
        else:
            act_fn(xs_copy(block, j, own))

    def xs_arrived(j, block, skip):
        source = source_of(j)
        ref = xs.at[source, block, :, pl.ds(skip, part - skip)]
        pltpu.make_async_remote_copy(
            src_ref=ref, dst_ref=ref,
            send_sem=xs_send.at[j, block], recv_sem=xs_recv.at[source, block],
            device_id={"rep": partner}, device_id_type=MESH,
        ).wait_recv()

    def xs_begin(block, piece):
        for j in reversed(range(1, n_rep)):
            @pl.when(source_of(j) // (n_rep // pieces) == piece)
            def _():
                xs_each(begin, block, j)

    def act_copy(target):
        return pltpu.make_async_remote_copy(
            src_ref=act_hbm, dst_ref=actg.at[rep],
            send_sem=act_send.at[target], recv_sem=act_recv.at[rep],
            device_id={"rep": target}, device_id_type=MESH,
        )

    def fw_copy(source):
        return pltpu.make_async_remote_copy(
            src_ref=actg.at[source], dst_ref=actg.at[source],
            send_sem=fw_send.at[source], recv_sem=act_recv.at[source],
            device_id={"rep": partner}, device_id_type=MESH,
        )

    def gs_copy(j):
        return pltpu.make_async_remote_copy(
            src_ref=gs.at[rep], dst_ref=gs.at[rep],
            send_sem=gs_send.at[j], recv_sem=gs_recv.at[rep],
            device_id={"rep": source_of(j)}, device_id_type=MESH,
        )

    if ext:
        ext_copy(1).start()
    ag_own(0, begin)
    for piece in range(1, pieces):
        ag_own(piece, begin)
    for j in reversed(range(1, n_rep)):
        xs_each(begin, me, j, True)
    for target in cross:
        act_copy(target).start()
    act_copy(partner).start()

    place_r = lax.broadcasted_iota(jnp.int32, (tok, LANES), 0)
    place_c = lax.broadcasted_iota(jnp.int32, (tok, LANES), 1)
    lane_of = jnp.where(place_c == place_r + lax.rem(me, per) * tok, 1.0, 0.0).astype(BF16)
    ids = ids_ref[...].astype(F32)
    gates = gate_ref[...]
    named_by = jnp.dot((ids + 1.0).astype(BF16), lane_of, preferred_element_type=F32)
    gate_by = jnp.dot(gates.astype(BF16), lane_of, preferred_element_type=F32)
    row = lax.broadcasted_iota(jnp.int32, (n_ep * sub, LANES), 0)
    line = jnp.where(lax.rem(row, sub) < loc, row // sub * loc + lax.rem(row, sub) + 1, -1)
    line = line.astype(F32)
    dense = jnp.zeros((n_ep * sub, LANES), F32)
    for k in range(topk):
        dense = jnp.where(line == named_by[k : k + 1, :], gate_by[k : k + 1, :], dense)
    dg[...] = dense.reshape(n_ep, sub, LANES)
    gg[me] = dg[me]
    for j in range(1, n_ep):
        rg_copy(j).start()

    def inside(z):
        return (z >= 0) & (z < outer)

    def lines(s):
        for piece in range(pieces):
            for way in (-1, 1):
                z = zi + way * s

                @pl.when(inside(z))
                def _():
                    ag_arrived(z * INNER + yi, piece)
                    ag_all(z, piece, begin, way < 0, way > 0)
                    xs_begin(z * INNER + yi, piece)

    def sides(z):
        for j in range(1, INNER):
            block = z * INNER + lax.rem(yi + j, INNER)
            for piece in range(pieces):
                ag_arrived(block, piece)
                xs_begin(block, piece)

    def back_copy(target):
        return pltpu.make_async_remote_copy(
            src_ref=yb.at[target], dst_ref=rb.at[me],
            send_sem=back_send.at[target], recv_sem=back_recv.at[me],
            device_id={"ep": target}, device_id_type=MESH,
        )

    def input_rows(s):
        side = lax.rem(yi + 1, INNER)
        first = s == 1
        slots = [
            (jnp.where(first, me, (zi - s + 1) * INNER + side), inside(zi - s + 1)),
            ((zi + s - 1) * INNER + side, inside(zi + s - 1)),
            ((zi - s) * INNER + yi, inside(zi - s)),
            ((zi + s) * INNER + yi, inside(zi + s)),
        ]
        some = functools.reduce(lambda a, b: a | b, [slot[1] for slot in slots])

        @pl.when(some)
        def _():
            any_block = slots[3][0]
            for block, valid in reversed(slots[:3]):
                any_block = jnp.where(valid, block, any_block)
            blocks = [jnp.where(valid, block, any_block) for block, valid in slots]
            x = jnp.concatenate([xg[block] for block in blocks], axis=0)
            for e in range(loc):
                y = jnp.dot(x, wv[e], preferred_element_type=F32).astype(BF16)
                for k, block in enumerate(blocks):
                    yb[block, e] = y[k * tok : (k + 1) * tok]
            for block, valid in slots:
                @pl.when(valid & (block != me))
                def _():
                    back_copy(block).start()

    group = min(GROUP, n_ep)
    tiles = group // per
    slots = per * cap
    b_r = lax.broadcasted_iota(jnp.int32, (LANES, LANES), 0)
    b_c = lax.broadcasted_iota(jnp.int32, (LANES, LANES), 1)
    before = jnp.where((b_r // tok == b_c // tok) & (b_r < b_c), 1.0, 0.0).astype(BF16)
    p_r = lax.broadcasted_iota(jnp.int32, (slots, LANES), 0)
    p_c = lax.broadcasted_iota(jnp.int32, (slots, LANES), 1)
    offset = (p_r - p_c // tok * cap).astype(F32)

    def scale_rows(source, g, place):
        for q in range(tiles):
            gate = gs[source, g * tiles + q]
            named = jnp.where(gate > 0.0, 1.0, 0.0)
            slot = jnp.dot(named.astype(BF16), before, preferred_element_type=F32)
            for e in range(loc):
                pick = jnp.where(offset == slot[e : e + 1, :], gate[e : e + 1, :], 0.0)
                start = pl.multiple_of((g * tiles + q) * slots, 16)
                saved = actg[source, e, pl.ds(start, slots), :]
                at[place, e, pl.ds(q * LANES, LANES)] = transposed_dot(
                    pick.astype(BF16), saved
                ).astype(BF16)

    def act_arrived(source):
        fw_copy(source).wait_recv()

    def gs_arrived(j):
        source = source_of(j)
        pltpu.make_async_remote_copy(
            src_ref=gs.at[source], dst_ref=gs.at[source],
            send_sem=gs_send.at[j], recv_sem=gs_recv.at[source],
            device_id={"rep": source}, device_id_type=MESH,
        ).wait_recv()

    pairs = tok * topk
    t_r = lax.broadcasted_iota(jnp.int32, (pairs, tok), 0) // topk
    t_c = lax.broadcasted_iota(jnp.int32, (pairs, tok), 1)
    spread = jnp.where(t_r == t_c, 1.0, 0.0).astype(BF16)
    k_r = lax.rem(lax.broadcasted_iota(jnp.int32, (pairs, topk), 0), topk)
    k_c = lax.broadcasted_iota(jnp.int32, (pairs, topk), 1)

    def pair_column(values):
        rows = lax.dot_general(
            spread, values.astype(BF16), (((1,), (1,)), ((), ())), preferred_element_type=F32
        )
        return jnp.sum(jnp.where(k_r == k_c, rows, 0.0), axis=1, keepdims=True)

    span = group * loc * tok
    s_r = lax.broadcasted_iota(jnp.int32, (pairs, span), 0) // topk
    s_c = lax.broadcasted_iota(jnp.int32, (pairs, span), 1)
    same_token = s_r == lax.rem(s_c, tok)
    s_e = (s_c // tok).astype(F32)

    def choose():
        pair_id = pair_column(ids)
        high = gates.astype(BF16).astype(F32)
        pair_gate[...] = pair_column(high) + pair_column(gates - high)
        for g in range(n_ep // group):
            mine = same_token & (s_e + float(g * group * loc) == pair_id)
            chosen[g] = jnp.where(mine, 1.0, 0.0).astype(BF16)

    @pl.loop(1, outer + 1)
    def _(s):
        lines(s)

        @pl.when(s == 1)
        def _():
            for j in range(1, n_ep):
                source = lax.rem(me + j, n_ep)
                pltpu.make_async_remote_copy(
                    src_ref=gg.at[source], dst_ref=gg.at[source],
                    send_sem=rg_send.at[j], recv_sem=rg_recv.at[source],
                    device_id={"ep": source}, device_id_type=MESH,
                ).wait_recv()
            gs[rep] = jnp.sum(gg[...].reshape(n_ep // per, per, sub, LANES), axis=1)
            for j in range(1, n_rep):
                gs_copy(j).start()
            load_x.wait()
            load_w.wait()
            sides(zi)

        @pl.when(s > 1)
        def _():
            for way in (-1, 1):
                z = zi + way * (s - 1)

                @pl.when(inside(z))
                def _():
                    sides(z)

        input_rows(s)

        @pl.when(s == 2)
        def _():
            choose()
            if early:
                load_a.wait()
                scale_rows(rep, 0, 0)
                act_arrived(partner)
                gs_arrived(1)
                scale_rows(partner, 0, 1)

        if ext:
            @pl.when((s == EXT_STEP) & helped)
            def _():
                for k in range(2):
                    ext_arrived(k)
                for j in range(1, n_ep):
                    xe_copy(j).start()

    own_y = pltpu.make_async_copy(yb.at[me], rb.at[me], lsem.at[3])
    own_y.start()
    if not early:
        load_a.wait()

    for source in cross:
        act_arrived(source)
        fw_copy(source).start()

    if not early:
        act_arrived(partner)
        gs_arrived(1)
    for j in range(2, n_rep):
        gs_arrived(j)

    def x_own(g):
        cols = pl.ds(pl.multiple_of(rep * part, LANES), part)
        return xg[pl.ds(g * group, group), :, cols].reshape(group * tok, part)

    def x_near(source, g):
        return xs[source, pl.ds(g * group, group)].reshape(group * tok, part)

    def x_late(first, count, skip):
        return jnp.concatenate([
            xs[source_of(j), pl.ds(first, count), :, pl.ds(skip, part - skip)].reshape(
                count * tok, part - skip
            )
            for j in range(2, n_rep)
        ], axis=0)

    def at_late(e, first, count):
        rows = pl.ds(pl.multiple_of(first * tok, LANES // 2), count * tok)
        return jnp.concatenate([at[j, e, rows, :] for j in range(2, n_rep)], axis=0)

    def x_ext(source):
        cols = pl.ds(pl.multiple_of(lax.rem(source, 2) * ext, LANES), ext)
        return xe[:, :, cols].reshape(n_ep * tok, ext)

    def wait_blocks(j, skip, first=0, count=n_ep):
        @pl.loop(0, count)
        def _(k):
            xs_arrived(j, first + k, skip)

    def settle():
        for j in range(1, n_ep):
            rg_copy(j).wait_send()
        if ext:
            ext_copy(1).wait_send()

            @pl.when(helped)
            def _():
                for j in range(1, n_ep):
                    xe_copy(j).wait_send()
        for piece in range(pieces):
            ag_own(piece, end_send)
        for s in range(1, outer):
            @pl.when(zi - s >= 0)
            def _():
                for piece in range(pieces):
                    ag_all(zi - s, piece, end_send, True, False)

            @pl.when(zi + s < outer)
            def _():
                for piece in range(pieces):
                    ag_all(zi + s, piece, end_send, False, True)
        for target in cross + [partner]:
            act_copy(target).wait_send()
        for j in range(1, n_rep):
            gs_copy(j).wait_send()
        for source in cross:
            fw_copy(source).wait_send()

    def settle_rows(first, count):
        @pl.loop(0, count)
        def _(k):
            for j in range(1, n_rep):
                xs_each(end_send, first + k, j)

    def settle_back():
        for j in range(1, n_ep):
            back_copy(lax.rem(me + j, n_ep)).wait_send()

    def far_products(skip):
        if skip:
            for j in range(1, n_ep):
                xe_arrived(lax.rem(me + j, n_ep))
            for e in range(loc):
                term = acc[e, pl.ds(0, skip)]
                for j in range(2, n_rep):
                    term += transposed_dot(x_ext(source_of(j)), at[j, e])
                wg_ref[e, pl.ds(0, skip)] = term.astype(BF16)
        rest = pl.ds(skip, part - skip)
        late = INNER
        soon = jnp.where(zi >= outer // 2, late, 0)
        last = jnp.where(zi >= outer // 2, 0, n_ep - late)
        settle()
        for first, count in ((soon, n_ep - late), (last, late)):
            if count == late:
                settle_rows(soon, n_ep - late)
                settle_back()
            for j in range(2, n_rep):
                wait_blocks(j, skip, first, count)
            if count == late:
                settle_rows(last, late)
            x_part = x_late(first, count, skip)
            for e in range(loc):
                total = acc[e, rest] + transposed_dot(x_part, at_late(e, first, count))
                if count == late:
                    wg_ref[e, rest] = total.astype(BF16)
                else:
                    acc[e, rest] = total

    if early:
        for e in range(loc):
            acc[e] = transposed_dot(x_own(0), at[0, e])
        wait_blocks(1, 0)
        for e in range(loc):
            acc[e] += transposed_dot(x_near(partner, 0), at[1, e])
        for j in range(2, n_rep):
            if j % 2:
                act_arrived(source_of(j))
            scale_rows(source_of(j), 0, j)
        if ext:
            for here, skip in ((helped, ext), (~helped, 0)):
                @pl.when(here)
                def _():
                    far_products(skip)
        else:
            far_products(0)
    else:
        acc[...] = jnp.zeros_like(acc)

        @pl.loop(0, n_ep // group)
        def _(g):
            scale_rows(rep, g, 0)
            for e in range(loc):
                acc[e] += transposed_dot(x_own(g), at[0, e])

        @pl.loop(1, n_rep)
        def _(j):
            source = source_of(j)

            @pl.when((j > 1) & (lax.rem(j, 2) == 1))
            def _():
                act_arrived(source)

            @pl.loop(0, n_ep)
            def _(block):
                pltpu.make_async_remote_copy(
                    src_ref=xs.at[source, block], dst_ref=xs.at[source, block],
                    send_sem=xs_send.at[j, block], recv_sem=xs_recv.at[source, block],
                    device_id={"rep": partner}, device_id_type=MESH,
                ).wait_recv()

            @pl.loop(0, n_ep // group)
            def _(g):
                scale_rows(source, g, 0)
                for e in range(loc):
                    acc[e] += transposed_dot(x_near(source, g), at[0, e])

        wg_ref[...] = acc[...].astype(BF16)

    own_y.wait()
    for j in range(1, n_ep):
        source = lax.rem(me + j, n_ep)
        pltpu.make_async_remote_copy(
            src_ref=yb.at[source], dst_ref=rb.at[source],
            send_sem=back_send.at[j], recv_sem=back_recv.at[source],
            device_id={"ep": source}, device_id_type=MESH,
        ).wait_recv()
    total = jnp.zeros((pairs, hid), F32)
    for g in range(n_ep // group):
        total += jnp.dot(
            chosen[g],
            rb[g * group : (g + 1) * group].reshape(span, hid),
            preferred_element_type=F32,
        )
    ing_ref[...] = (total * pair_gate[...]).astype(ing_ref.dtype)

    if not early:
        settle()
        settle_rows(0, n_ep)
        settle_back()


def finish(in_v, w_v, in_out, w_out, sem):
    loc = w_v.shape[0]
    pairs = [(w_v.at[e], w_out.at[e]) for e in range(loc)] + [(in_v, in_out)]
    stores = [pltpu.make_async_copy(p[0], p[1], sem.at[k]) for k, p in enumerate(pairs)]
    for store in stores:
        store.start()
    for store in stores:
        store.wait()


def shards(out_grad, gate_weights, expert_ids, down_weight, act_cache):
    n_ep, n_rep = lax.axis_size("ep"), lax.axis_size("rep")
    tok, topk = expert_ids.shape
    loc, model, hid = down_weight.shape
    part = model // n_rep
    early = n_ep <= GROUP
    pieces = PIECES if early else 1
    ext = part // (4 * LANES) * LANES if n_rep == 4 and early else 0
    sub = pl.cdiv(loc, 8) * 8
    per = LANES // tok
    dma = pltpu.SemaphoreType.DMA
    vmem = pl.BlockSpec(memory_space=pltpu.VMEM)
    hbm = pl.BlockSpec(memory_space=pl.ANY)
    in_grad, weight_grad = pl.pallas_call(
        functools.partial(kernel, n_ep, n_rep, ext, pieces),
        out_shape=(
            pltpu.VMEM((tok * topk, hid), BF16),
            pltpu.VMEM((loc, part, hid), BF16),
        ),
        in_specs=[hbm, vmem, vmem, hbm, hbm],
        out_specs=(vmem, vmem),
        scratch_shapes=[
            pltpu.VMEM((n_ep, tok, model), BF16),
            pltpu.VMEM((n_ep, tok, max(2 * ext, LANES)), BF16),
            pltpu.VMEM((n_rep, n_ep, tok, part), BF16),
            pltpu.VMEM((n_ep, sub, LANES), F32),
            pltpu.VMEM((n_ep, sub, LANES), F32),
            pltpu.VMEM((n_rep, n_ep // per, sub, LANES), F32),
            pltpu.VMEM((n_rep,) + act_cache.shape, BF16),
            pltpu.VMEM((loc, model, hid), BF16),
            pltpu.VMEM((n_ep, loc, tok, hid), BF16),
            pltpu.VMEM((n_ep, loc, tok, hid), BF16),
            pltpu.VMEM((loc, part, hid), F32),
            pltpu.VMEM((n_rep if early else 1, loc, min(GROUP, n_ep) * tok, hid), BF16),
            pltpu.VMEM((n_ep // min(GROUP, n_ep), tok * topk, min(GROUP, n_ep) * loc * tok), BF16),
            pltpu.VMEM((tok * topk, 1), F32),
            dma((4,)), dma((1 + INNER, n_ep, pieces)), dma((n_ep, pieces)),
            dma((2,)), dma((2,)), dma((n_ep,)), dma((n_ep,)),
            dma((n_ep,)), dma((n_ep,)),
            dma((n_rep,)), dma((n_rep,)), dma((n_rep,)),
            dma((n_rep,)), dma((n_rep,)),
            dma((n_rep, n_ep)), dma((n_rep, n_ep)),
            dma((n_ep,)), dma((n_ep,)),
        ],
        compiler_params=pltpu.CompilerParams(
            collective_id=0, has_side_effects=True, vmem_limit_bytes=60 * 1024 * 1024
        ),
    )(out_grad, expert_ids.T, gate_weights.T, down_weight, act_cache)
    in_grad, weight_grad = pl.pallas_call(
        finish,
        out_shape=(
            jax.ShapeDtypeStruct((tok * topk, hid), BF16),
            jax.ShapeDtypeStruct((loc, part, hid), BF16),
        ),
        in_specs=[vmem, vmem],
        out_specs=(hbm, hbm),
        scratch_shapes=[dma((1 + loc,))],
        compiler_params=pltpu.CompilerParams(vmem_limit_bytes=1024 * 1024),
    )(
        pltpu.with_memory_space_constraint(in_grad, pltpu.VMEM),
        pltpu.with_memory_space_constraint(weight_grad, pltpu.VMEM),
    )
    return in_grad.reshape(tok, topk, hid), weight_grad


def solution(mesh):
    in_specs = (
        P(("ep", "rep"), None),
        P(("ep", "rep"), None),
        P(("ep", "rep"), None),
        P("ep", None, None),
        P("ep", "rep", None),
    )
    out_specs = (P(("ep", "rep"), None, None), P("ep", "rep", None))
    return jax.shard_map(shards, mesh=mesh, in_specs=in_specs, out_specs=out_specs, check_vma=False)
```
